512 devices in a mesh: ctx: 64 (over x, z), tp: 8 (over y, core).
Axes of the slice: x: 4, y: 4, z: 16, core: 2. Of those that a mesh axis runs over, the one named last changes fastest.
Arguments:
- section_token_rows: bfloat16 [32768, 7168], P(('ctx', 'tp')), may hold values from -6 to 6
- row_target: int32 [32768], P(('ctx', 'tp')), may hold values from 0 to 32767, as said below
- doc_lengths: int32 [128], replicated, may hold values from 1 to 512, as said below
Outputs:
- attn_out: bfloat16 [32768, 5120], P(('ctx', 'tp'))
The draws below stay inside these ranges and needn't reach their ends.
Inputs may be any that keep to these rules, and one draw needn't show every extreme that they name: row_target is a permutation of the 32768 pack positions; for every block of 512 consecutive previous-section rows and every block of 512 consecutive pack positions, exactly 8 rows of the first go to the second. `doc_lengths`: the lengths sum to 32768; the longest is exactly 512.
All inputs are finite; a program needn't handle non-finite values.
Results may differ from the reference program's by a relative error of at most 0.0029.
Values may be sent and summed in bfloat16 or wider, within the bound.
No kernel may reach another device: no remote copies, remote signals or barrier semaphores. Data moves between devices by JAX's collectives and lax.ppermute only.
A program may use at most 64 MiB of HBM per device.

```python
import math
import jax
import jax.numpy as jnp
from jax import lax

HQ = 40
KEY_VALUE_HEADS = 8
HEAD_SIZE = 128
QUERY_PER_KEY = 5
QKVW = 7168
TOKENS_PER_SLICE = 512
PACK_TOKENS = 32768
MAXDOC = 512
DOCS = 128


def plan_targets(key):
    group_count = PACK_TOKENS // TOKENS_PER_SLICE
    per_pair = TOKENS_PER_SLICE // group_count
    plan_key = jax.random.fold_in(key, 11)
    place_keys = jax.random.split(jax.random.fold_in(plan_key, 1), group_count)
    order_keys = jax.random.split(jax.random.fold_in(plan_key, 2), group_count)
    placing = jax.vmap(lambda one_key: jax.random.permutation(one_key, TOKENS_PER_SLICE))(place_keys)
    sending = jax.vmap(lambda one_key: jax.random.permutation(one_key, TOKENS_PER_SLICE))(order_keys)
    source = jnp.arange(group_count, dtype=jnp.int32)[:, None]
    sent_slot = jnp.arange(TOKENS_PER_SLICE, dtype=jnp.int32)[None, :]
    destination = sent_slot // per_pair
    within = sent_slot % per_pair
    chosen = placing[destination, source * per_pair + within]
    target_value = (destination * TOKENS_PER_SLICE + chosen).astype(jnp.int32)
    row_index = (source * TOKENS_PER_SLICE + sending).astype(jnp.int32)
    return jnp.zeros((PACK_TOKENS,), jnp.int32).at[row_index.reshape(-1)].set(target_value.reshape(-1))


def plan_lengths(key):
    plan_key = jax.random.fold_in(key, 23)
    remain = PACK_TOKENS - MAXDOC
    common = remain // (DOCS - 1)
    leftover = remain - common * (DOCS - 1)
    wiggle = jax.random.randint(jax.random.fold_in(plan_key, 1), (DOCS - 1,), 0, TOKENS_PER_SLICE // 4 + 1)
    index_rest = jnp.arange(DOCS - 1, dtype=jnp.int32)
    others = common + (index_rest < leftover).astype(jnp.int32) + wiggle - jnp.roll(wiggle, -1)
    long_at = jax.random.randint(jax.random.fold_in(plan_key, 2), (), 0, DOCS)
    every_doc = jnp.arange(DOCS, dtype=jnp.int32)
    moved = jnp.clip(jnp.where(every_doc < long_at, every_doc, every_doc - 1), 0, DOCS - 2)
    return jnp.where(every_doc == long_at, MAXDOC, others[moved]).astype(jnp.int32)


def draw_row_target(key, part):
    return plan_targets(key)


def draw_doc_lengths(key, part):
    return plan_lengths(key)


def draw_section_token_rows(key, part):
    random_noise_key = jax.random.fold_in(key, 37)
    return jnp.clip(jax.random.normal(jax.random.fold_in(random_noise_key, 4), (PACK_TOKENS, QKVW)), -6.0, 6.0).astype(jnp.bfloat16)


def setup_inputs(seed: int = 0) -> dict:
    key_of = jax.random.split(jax.random.key(seed), 4)
    return {
        "section_token_rows": draw_section_token_rows(jax.random.fold_in(key_of[3], 71), 0),
        "row_target": draw_row_target(jax.random.fold_in(key_of[3], 71), 0),
        "doc_lengths": draw_doc_lengths(jax.random.fold_in(key_of[3], 71), 0),
    }


def reference(section_token_rows, row_target, doc_lengths):
    packed_tokens = jnp.zeros_like(section_token_rows).at[row_target].set(section_token_rows)
    divided_rows = packed_tokens.reshape(PACK_TOKENS, KEY_VALUE_HEADS, QUERY_PER_KEY + 2, HEAD_SIZE)
    queries = divided_rows[:, :, :QUERY_PER_KEY]
    key_rows = divided_rows[:, :, QUERY_PER_KEY]
    value_rows = divided_rows[:, :, QUERY_PER_KEY + 1]
    empty_rows = jnp.zeros((TOKENS_PER_SLICE, KEY_VALUE_HEADS, HEAD_SIZE), section_token_rows.dtype)
    key_padded = jnp.concatenate([empty_rows, key_rows], axis=0)
    value_padded = jnp.concatenate([empty_rows, value_rows], axis=0)
    positions = jnp.arange(PACK_TOKENS, dtype=jnp.int32)
    doc_ends = jnp.cumsum(doc_lengths)
    doc_starts = doc_ends - doc_lengths
    starts = lax.optimization_barrier(jnp.max(jnp.where(doc_starts[None, :] <= positions[:, None], doc_starts[None, :], 0), axis=1))
    score_scale = 1.0 / math.sqrt(HEAD_SIZE)

    def one_block(block_at):
        first_row = (block_at * TOKENS_PER_SLICE).astype(jnp.int32)
        block_q = lax.dynamic_slice_in_dim(queries, first_row, TOKENS_PER_SLICE, 0).astype(jnp.float32)
        block_k = lax.dynamic_slice_in_dim(key_padded, first_row, 2 * TOKENS_PER_SLICE, 0).astype(jnp.float32)
        block_v = lax.dynamic_slice_in_dim(value_padded, first_row, 2 * TOKENS_PER_SLICE, 0).astype(jnp.float32)
        query_pos = first_row + jnp.arange(TOKENS_PER_SLICE, dtype=jnp.int32)
        key_pos = first_row - TOKENS_PER_SLICE + jnp.arange(2 * TOKENS_PER_SLICE, dtype=jnp.int32)
        block_starts = lax.dynamic_slice_in_dim(starts, first_row, TOKENS_PER_SLICE, 0)
        allowed = (key_pos[None, :] >= block_starts[:, None]) & (key_pos[None, :] <= query_pos[:, None])
        scores = jnp.einsum('qhgd,khd->hgqk', block_q, block_k) * score_scale
        scores = jnp.where(allowed[None, None], scores, -jnp.inf)
        row_max = lax.optimization_barrier(jnp.max(scores, axis=-1, keepdims=True))
        weights = jnp.exp(scores - row_max)
        row_total = lax.optimization_barrier(jnp.sum(weights, axis=-1, keepdims=True))
        rounded = lax.optimization_barrier(weights.astype(jnp.bfloat16)).astype(jnp.float32)
        weighted = jnp.einsum('hgqk,khd->hgqd', rounded, block_v) / row_total
        return jnp.transpose(weighted, (2, 0, 1, 3)).reshape(TOKENS_PER_SLICE, HQ * HEAD_SIZE).astype(jnp.bfloat16)
    attended = lax.map(one_block, jnp.arange(PACK_TOKENS // TOKENS_PER_SLICE, dtype=jnp.int32))
    attended = attended.reshape(PACK_TOKENS, HQ * HEAD_SIZE)
    return attended[row_target]
```

```python
import functools
import math

import jax
import jax.numpy as jnp
from jax import lax
from jax.experimental import pallas as pl
from jax.experimental.pallas import tpu as pltpu
from jax.sharding import PartitionSpec as P

HEAD_SIZE = 128
QUERY_PER_KEY = 5
LANES = 128
QUERY_WIDTH = QUERY_PER_KEY * HEAD_SIZE
KV_WIDTH = 2 * HEAD_SIZE
KEY_CHUNK = KV_WIDTH + LANES
MASKED = -1e30
QUERY_ROWS = 128
VMEM_LIMIT = 24 * 1024 * 1024


def whole(n):
    return [pl.BlockSpec(memory_space=pltpu.VMEM)] * n


def params():
    return pltpu.CompilerParams(vmem_limit_bytes=VMEM_LIMIT)


def cost(flops, moved):
    return pl.CostEstimate(flops=flops, bytes_accessed=moved, transcendentals=0)


def eye(n):
    return lax.broadcasted_iota(jnp.int32, (n, n), 0) == lax.broadcasted_iota(jnp.int32, (n, n), 1)


def column_to_row(column):
    n = column.shape[0]
    return jnp.sum(jnp.where(eye(n), column, 0.0), axis=0, keepdims=True)


def position_column(chunk_ref):
    high = chunk_ref[:, KV_WIDTH : KV_WIDTH + LANES].astype(jnp.float32)
    return high[:, 0:1] * 256.0 + high[:, 1:2]


def split_kernel(target_ref, rows_ref, keys_ref, queries_ref):
    n = rows_ref.shape[0]
    target = jnp.sum(jnp.where(eye(n), target_ref[...], 0), axis=1, keepdims=True)
    lane = lax.broadcasted_iota(jnp.int32, (n, LANES), 1)
    coded = jnp.where(lane == 0, target >> 8, jnp.where(lane == 1, target & 255, 0))
    queries_ref[0] = rows_ref[:, :QUERY_WIDTH]
    keys_ref[0, :, :KV_WIDTH] = rows_ref[:, QUERY_WIDTH:]
    keys_ref[0, :, KV_WIDTH:] = coded.astype(jnp.float32).astype(jnp.bfloat16)


def split_rows(rows, target, groups):
    n, width = rows.shape
    return pl.pallas_call(
        split_kernel,
        grid=(groups,),
        in_specs=[
            pl.BlockSpec((1, n), lambda g: (0, 0)),
            pl.BlockSpec((n, width // groups), lambda g: (0, g)),
        ],
        out_specs=[
            pl.BlockSpec((1, n, KEY_CHUNK), lambda g: (g, 0, 0)),
            pl.BlockSpec((1, n, QUERY_WIDTH), lambda g: (g, 0, 0)),
        ],
        out_shape=[
            jax.ShapeDtypeStruct((groups, n, KEY_CHUNK), rows.dtype),
            jax.ShapeDtypeStruct((groups, n, QUERY_WIDTH), rows.dtype),
        ],
        compiler_params=params(),
        cost_estimate=cost(0, 2 * rows.size * 2),
        name="split_rows",
    )(target.reshape(1, n), rows)


def sort_kernel(chunk_ref, sorted_ref, forward_ref, backward_ref):
    n = chunk_ref.shape[0]
    column = position_column(chunk_ref)
    row = column_to_row(column)
    rank_row = jnp.sum(jnp.where(column < row, 1.0, 0.0), axis=0, keepdims=True)
    rank_column = jnp.sum(jnp.where(row < column, 1.0, 0.0), axis=1, keepdims=True)
    down = lax.broadcasted_iota(jnp.int32, (n, n), 0).astype(jnp.float32)
    across = lax.broadcasted_iota(jnp.int32, (n, n), 1).astype(jnp.float32)
    forward = jnp.where(rank_row == down, 1.0, 0.0).astype(jnp.bfloat16)
    forward_ref[...] = forward
    backward_ref[...] = jnp.where(rank_column == across, 1.0, 0.0).astype(jnp.bfloat16)
    sorted_ref[...] = jnp.dot(
        forward, chunk_ref[...], preferred_element_type=jnp.float32
    ).astype(sorted_ref.dtype)


def sort_chunk(chunk):
    n = chunk.shape[0]
    return pl.pallas_call(
        sort_kernel,
        in_specs=whole(1),
        out_specs=whole(3),
        out_shape=[
            jax.ShapeDtypeStruct(chunk.shape, chunk.dtype),
            jax.ShapeDtypeStruct((n, n), jnp.bfloat16),
            jax.ShapeDtypeStruct((n, n), jnp.bfloat16),
        ],
        compiler_params=params(),
        cost_estimate=cost(2 * n * chunk.size, 4 * chunk.size),
        name="sort_chunk",
    )(chunk)


def permute_kernel(order_ref, chunk_ref, out_ref):
    out_ref[...] = jnp.dot(
        order_ref[...], chunk_ref[...], preferred_element_type=jnp.float32
    ).astype(out_ref.dtype)


def permute_rows(order, chunk, name):
    return pl.pallas_call(
        permute_kernel,
        in_specs=whole(2),
        out_specs=pl.BlockSpec(memory_space=pltpu.VMEM),
        out_shape=jax.ShapeDtypeStruct(chunk.shape, chunk.dtype),
        compiler_params=params(),
        cost_estimate=cost(2 * chunk.shape[0] * chunk.size, 4 * chunk.size),
        name=name,
    )(order, chunk)


def attend_kernel(heads, starts_ref, own_ref, earlier_ref, query_ref, out_ref, bias_ref):
    n = own_ref.shape[0]
    own_column = position_column(own_ref)
    own_row = column_to_row(own_column)
    earlier_row = column_to_row(position_column(earlier_ref))
    starts = starts_ref[...].astype(jnp.float32)
    start = jnp.max(jnp.where(starts <= own_column, starts, 0.0), axis=1, keepdims=True)
    for half, keys in enumerate((earlier_row, own_row)):
        allowed = (keys >= start) & (keys <= own_column)
        bias_ref[:, half * n : (half + 1) * n] = jnp.where(allowed, 0.0, MASKED)
    scale = math.log2(math.e) / math.sqrt(HEAD_SIZE)
    keys = jnp.concatenate([earlier_ref[:, :HEAD_SIZE], own_ref[:, :HEAD_SIZE]], axis=0)
    values = jnp.concatenate(
        [earlier_ref[:, HEAD_SIZE:KV_WIDTH], own_ref[:, HEAD_SIZE:KV_WIDTH]], axis=0
    )
    for at, head in enumerate(heads):
        for first in range(0, n, QUERY_ROWS):
            rows = slice(first, first + QUERY_ROWS)
            query = query_ref[rows, head * HEAD_SIZE : (head + 1) * HEAD_SIZE]
            scores = lax.dot_general(
                query, keys, (((1,), (1,)), ((), ())), preferred_element_type=jnp.float32
            )
            scores = scores * scale + bias_ref[rows, :]
            weights = jnp.exp2(scores - jnp.max(scores, axis=1, keepdims=True))
            total = jnp.sum(weights, axis=1, keepdims=True)
            weighted = jnp.dot(
                weights.astype(jnp.bfloat16), values, preferred_element_type=jnp.float32
            )
            out_ref[rows, at * HEAD_SIZE : (at + 1) * HEAD_SIZE] = (weighted / total).astype(
                out_ref.dtype
            )


def attend(heads, starts, own, earlier, queries):
    n = own.shape[0]
    width = len(heads) * HEAD_SIZE
    return pl.pallas_call(
        functools.partial(attend_kernel, heads),
        in_specs=whole(4),
        out_specs=pl.BlockSpec(memory_space=pltpu.VMEM),
        out_shape=jax.ShapeDtypeStruct((n, width), own.dtype),
        scratch_shapes=[pltpu.VMEM((n, 2 * n), jnp.float32)],
        compiler_params=params(),
        cost_estimate=cost(8 * n * n * width, 2 * (2 * own.size + 2 * n * width)),
        name="attend",
    )(starts, own, earlier, queries)


def join_kernel(*refs):
    out_ref = refs[-1]
    at = 0
    for ref in refs[:-1]:
        out_ref[:, at : at + ref.shape[2]] = ref[0]
        at += ref.shape[2]


def join_groups(pieces):
    groups, n, _ = pieces[0].shape
    widths = [piece.shape[2] for piece in pieces]
    return pl.pallas_call(
        join_kernel,
        grid=(groups,),
        in_specs=[pl.BlockSpec((1, n, w), lambda g: (g, 0, 0)) for w in widths],
        out_specs=pl.BlockSpec((n, sum(widths)), lambda g: (0, g)),
        out_shape=jax.ShapeDtypeStruct((n, groups * sum(widths)), pieces[0].dtype),
        compiler_params=params(),
        cost_estimate=cost(0, 4 * groups * n * sum(widths)),
        name="join_groups",
    )(*pieces)


def exchange(blocks, axis):
    return lax.all_to_all(blocks, axis, split_axis=0, concat_axis=0, tiled=True)


OUT_CHUNKS = ((0, 1), (2, 3, 4))


def per_device(section_token_rows, row_target, doc_lengths):
    tp_count = lax.axis_size("tp")
    ctx_count = lax.axis_size("ctx")
    local_rows = section_token_rows.shape[0]
    tok_dev = local_rows * tp_count
    per_pair = tok_dev // ctx_count
    starts = (jnp.cumsum(doc_lengths) - doc_lengths).reshape(1, -1)

    keys_out, queries_out = split_rows(section_token_rows, row_target, tp_count)
    keys_in = exchange(keys_out, "tp").reshape(tok_dev, KEY_CHUNK)
    queries_in = exchange(queries_out, "tp").reshape(tok_dev, QUERY_WIDTH)
    keys_sorted, forward, backward = sort_chunk(keys_in)
    queries_sorted = permute_rows(forward, queries_in, "sort_queries")

    own = exchange(keys_sorted.reshape(ctx_count, per_pair, KEY_CHUNK), "ctx")
    own = own.reshape(tok_dev, KEY_CHUNK)
    queries = exchange(queries_sorted.reshape(ctx_count, per_pair, QUERY_WIDTH), "ctx")
    queries = queries.reshape(tok_dev, QUERY_WIDTH)
    route = [(i, (i + 1) % ctx_count) for i in range(ctx_count)]
    earlier = lax.ppermute(own, "ctx", route)

    pieces = []
    for heads in OUT_CHUNKS:
        done = attend(heads, starts, own, earlier, queries)
        width = done.shape[1]
        back = exchange(done.reshape(ctx_count, per_pair, width), "ctx").reshape(tok_dev, width)
        back = permute_rows(backward, back, "unsort")
        pieces.append(exchange(back.reshape(tp_count, local_rows, width), "tp"))
    return join_groups(pieces)


def solution(mesh):
    placed = (P(("ctx", "tp"), None), P(("ctx", "tp")), P())
    return jax.shard_map(
        per_device, mesh=mesh, in_specs=placed, out_specs=P(("ctx", "tp"), None), check_vma=False
    )
```

```python
import functools
import math

import jax
import jax.numpy as jnp
from jax import lax
from jax.experimental import pallas as pl
from jax.experimental.pallas import tpu as pltpu
from jax.sharding import PartitionSpec as P

HEAD_SIZE = 128
QUERY_PER_KEY = 5
LANES = 128
QUERY_WIDTH = QUERY_PER_KEY * HEAD_SIZE
KV_WIDTH = 2 * HEAD_SIZE
WIDTH = KV_WIDTH + LANES + QUERY_WIDTH
QUERIES_AT = KV_WIDTH + LANES
MASKED = -1e30
QUERY_ROWS = 128
VMEM_LIMIT = 24 * 1024 * 1024


def whole(n):
    return [pl.BlockSpec(memory_space=pltpu.VMEM)] * n


def params():
    return pltpu.CompilerParams(vmem_limit_bytes=VMEM_LIMIT)


def cost(flops, moved):
    return pl.CostEstimate(flops=flops, bytes_accessed=moved, transcendentals=0)


def eye(n):
    return lax.broadcasted_iota(jnp.int32, (n, n), 0) == lax.broadcasted_iota(jnp.int32, (n, n), 1)


def column_to_row(column):
    n = column.shape[0]
    return jnp.sum(jnp.where(eye(n), column, 0.0), axis=0, keepdims=True)


def position_column(chunk_ref):
    high = chunk_ref[:, KV_WIDTH : KV_WIDTH + LANES].astype(jnp.float32)
    return high[:, 0:1] * 256.0 + high[:, 1:2]


def split_kernel(target_ref, rows_ref, out_ref):
    n = rows_ref.shape[0]
    target = jnp.sum(jnp.where(eye(n), target_ref[...], 0), axis=1, keepdims=True)
    lane = lax.broadcasted_iota(jnp.int32, (n, LANES), 1)
    coded = jnp.where(lane == 0, target >> 8, jnp.where(lane == 1, target & 255, 0))
    out_ref[0, :, QUERIES_AT:] = rows_ref[:, :QUERY_WIDTH]
    out_ref[0, :, :KV_WIDTH] = rows_ref[:, QUERY_WIDTH:]
    out_ref[0, :, KV_WIDTH:QUERIES_AT] = coded.astype(jnp.float32).astype(jnp.bfloat16)


def split_rows(rows, target, groups):
    n, width = rows.shape
    return pl.pallas_call(
        split_kernel,
        grid=(groups,),
        in_specs=[
            pl.BlockSpec((1, n), lambda g: (0, 0)),
            pl.BlockSpec((n, width // groups), lambda g: (0, g)),
        ],
        out_specs=pl.BlockSpec((1, n, WIDTH), lambda g: (g, 0, 0)),
        out_shape=jax.ShapeDtypeStruct((groups, n, WIDTH), rows.dtype),
        compiler_params=params(),
        cost_estimate=cost(0, 2 * rows.size * 2),
        name="split_rows",
    )(target.reshape(1, n), rows)


def sort_kernel(chunk_ref, sorted_ref, backward_ref):
    n = chunk_ref.shape[0]
    column = position_column(chunk_ref)
    row = column_to_row(column)
    rank_row = jnp.sum(jnp.where(column < row, 1.0, 0.0), axis=0, keepdims=True)
    rank_column = jnp.sum(jnp.where(row < column, 1.0, 0.0), axis=1, keepdims=True)
    down = lax.broadcasted_iota(jnp.int32, (n, n), 0).astype(jnp.float32)
    across = lax.broadcasted_iota(jnp.int32, (n, n), 1).astype(jnp.float32)
    forward = jnp.where(rank_row == down, 1.0, 0.0).astype(jnp.bfloat16)
    backward_ref[...] = jnp.where(rank_column == across, 1.0, 0.0).astype(jnp.bfloat16)
    sorted_ref[...] = jnp.dot(
        forward, chunk_ref[...], preferred_element_type=jnp.float32
    ).astype(sorted_ref.dtype)


def sort_chunk(chunk):
    n = chunk.shape[0]
    return pl.pallas_call(
        sort_kernel,
        in_specs=whole(1),
        out_specs=whole(2),
        out_shape=[
            jax.ShapeDtypeStruct(chunk.shape, chunk.dtype),
            jax.ShapeDtypeStruct((n, n), jnp.bfloat16),
        ],
        compiler_params=params(),
        cost_estimate=cost(2 * n * chunk.size, 4 * chunk.size),
        name="sort_chunk",
    )(chunk)


def permute_kernel(order_ref, chunk_ref, out_ref):
    out_ref[...] = jnp.dot(
        order_ref[...], chunk_ref[...], preferred_element_type=jnp.float32
    ).astype(out_ref.dtype)


def permute_rows(order, chunk, name):
    return pl.pallas_call(
        permute_kernel,
        in_specs=whole(2),
        out_specs=pl.BlockSpec(memory_space=pltpu.VMEM),
        out_shape=jax.ShapeDtypeStruct(chunk.shape, chunk.dtype),
        compiler_params=params(),
        cost_estimate=cost(2 * chunk.shape[0] * chunk.size, 4 * chunk.size),
        name=name,
    )(order, chunk)


def attend_kernel(heads, starts_ref, own_ref, earlier_ref, out_ref, bias_ref):
    n = own_ref.shape[0]
    own_column = position_column(own_ref)
    own_row = column_to_row(own_column)
    earlier_row = column_to_row(position_column(earlier_ref))
    starts = starts_ref[...].astype(jnp.float32)
    start = jnp.max(jnp.where(starts <= own_column, starts, 0.0), axis=1, keepdims=True)
    for half, keys in enumerate((earlier_row, own_row)):
        allowed = (keys >= start) & (keys <= own_column)
        bias_ref[:, half * n : (half + 1) * n] = jnp.where(allowed, 0.0, MASKED)
    scale = math.log2(math.e) / math.sqrt(HEAD_SIZE)
    keys = jnp.concatenate([earlier_ref[:, :HEAD_SIZE], own_ref[:, :HEAD_SIZE]], axis=0)
    values = jnp.concatenate(
        [earlier_ref[:, HEAD_SIZE:KV_WIDTH], own_ref[:, HEAD_SIZE:KV_WIDTH]], axis=0
    )
    for at, head in enumerate(heads):
        for first in range(0, n, QUERY_ROWS):
            rows = slice(first, first + QUERY_ROWS)
            at_column = QUERIES_AT + head * HEAD_SIZE
            query = own_ref[rows, at_column : at_column + HEAD_SIZE]
            scores = lax.dot_general(
                query, keys, (((1,), (1,)), ((), ())), preferred_element_type=jnp.float32
            )
            scores = scores * scale + bias_ref[rows, :]
            weights = jnp.exp2(scores - jnp.max(scores, axis=1, keepdims=True))
            total = jnp.sum(weights, axis=1, keepdims=True)
            weighted = jnp.dot(
                weights.astype(jnp.bfloat16), values, preferred_element_type=jnp.float32
            )
            out_ref[rows, at * HEAD_SIZE : (at + 1) * HEAD_SIZE] = (weighted / total).astype(
                out_ref.dtype
            )


def attend(heads, starts, own, earlier):
    n = own.shape[0]
    width = len(heads) * HEAD_SIZE
    return pl.pallas_call(
        functools.partial(attend_kernel, heads),
        in_specs=whole(3),
        out_specs=pl.BlockSpec(memory_space=pltpu.VMEM),
        out_shape=jax.ShapeDtypeStruct((n, width), own.dtype),
        scratch_shapes=[pltpu.VMEM((n, 2 * n), jnp.float32)],
        compiler_params=params(),
        cost_estimate=cost(8 * n * n * width, 2 * (2 * own.size + 2 * n * width)),
        name="attend",
    )(starts, own, earlier)


def join_kernel(*refs):
    out_ref = refs[-1]
    at = 0
    for ref in refs[:-1]:
        out_ref[:, at : at + ref.shape[2]] = ref[0]
        at += ref.shape[2]


def join_groups(pieces):
    groups, n, _ = pieces[0].shape
    widths = [piece.shape[2] for piece in pieces]
    return pl.pallas_call(
        join_kernel,
        grid=(groups,),
        in_specs=[pl.BlockSpec((1, n, w), lambda g: (g, 0, 0)) for w in widths],
        out_specs=pl.BlockSpec((n, sum(widths)), lambda g: (0, g)),
        out_shape=jax.ShapeDtypeStruct((n, groups * sum(widths)), pieces[0].dtype),
        compiler_params=params(),
        cost_estimate=cost(0, 4 * groups * n * sum(widths)),
        name="join_groups",
    )(*pieces)


def exchange(blocks, axis):
    return lax.all_to_all(blocks, axis, split_axis=0, concat_axis=0, tiled=True)


OUT_CHUNKS = ((0, 1, 2, 3, 4),)


def per_device(section_token_rows, row_target, doc_lengths):
    tp_count = lax.axis_size("tp")
    ctx_count = lax.axis_size("ctx")
    local_rows = section_token_rows.shape[0]
    tok_dev = local_rows * tp_count
    per_pair = tok_dev // ctx_count
    starts = (jnp.cumsum(doc_lengths) - doc_lengths).reshape(1, -1)

    rows = split_rows(section_token_rows, row_target, tp_count)
    rows = exchange(rows, "tp").reshape(tok_dev, WIDTH)
    rows, backward = sort_chunk(rows)
    own = exchange(rows.reshape(ctx_count, per_pair, WIDTH), "ctx").reshape(tok_dev, WIDTH)
    route = [(i, (i + 1) % ctx_count) for i in range(ctx_count)]
    earlier = lax.ppermute(own[:, :QUERIES_AT], "ctx", route)

    pieces = []
    for heads in OUT_CHUNKS:
        done = attend(heads, starts, own, earlier)
        width = done.shape[1]
        back = exchange(done.reshape(ctx_count, per_pair, width), "ctx").reshape(tok_dev, width)
        back = permute_rows(backward, back, "unsort")
        pieces.append(exchange(back.reshape(tp_count, local_rows, width), "tp"))
    return join_groups(pieces)


def solution(mesh):
    placed = (P(("ctx", "tp"), None), P(("ctx", "tp")), P())
    return jax.shard_map(
        per_device, mesh=mesh, in_specs=placed, out_specs=P(("ctx", "tp"), None), check_vma=False
    )
```

```python
import functools
import math

import jax
import jax.numpy as jnp
from jax import lax
from jax.experimental import pallas as pl
from jax.experimental.pallas import tpu as pltpu
from jax.sharding import Mesh
from jax.sharding import PartitionSpec as P

HEAD_SIZE = 128
QUERY_PER_KEY = 5
LANES = 128
BLOCK = 512
QUERY_WIDTH = QUERY_PER_KEY * HEAD_SIZE
KV_WIDTH = 2 * HEAD_SIZE
KEY_CHUNK = KV_WIDTH + LANES
MASKED = -1e30
VMEM_LIMIT = 24 * 1024 * 1024
AXES = ("x", "zh", "zl", "tp")
PART = ("x", "zl")
RING = ("zh", "zl")


def whole(n):
    return [pl.BlockSpec(memory_space=pltpu.VMEM)] * n


def params():
    return pltpu.CompilerParams(vmem_limit_bytes=VMEM_LIMIT)


def cost(flops, moved):
    return pl.CostEstimate(flops=flops, bytes_accessed=moved, transcendentals=0)


def iota(shape, axis):
    return lax.broadcasted_iota(jnp.int32, shape, axis)


def eye(n):
    return iota((n, n), 0) == iota((n, n), 1)


def column_to_row(column):
    n = column.shape[0]
    return jnp.sum(jnp.where(eye(n), column, 0.0), axis=0, keepdims=True)


def split_kernel(target_ref, rows_ref, keys_ref, queries_ref):
    n = rows_ref.shape[0]
    target = jnp.sum(jnp.where(eye(n), target_ref[...], 0), axis=1, keepdims=True)
    lane = iota((n, LANES), 1)
    coded = jnp.where(lane == 0, target >> 8, jnp.where(lane == 1, target & 255, 0))
    queries_ref[0] = rows_ref[:, :QUERY_WIDTH]
    keys_ref[0, :, :KV_WIDTH] = rows_ref[:, QUERY_WIDTH:]
    keys_ref[0, :, KV_WIDTH:] = coded.astype(jnp.float32).astype(jnp.bfloat16)


def split_rows(rows, target, groups):
    n, width = rows.shape
    return pl.pallas_call(
        split_kernel,
        grid=(groups,),
        in_specs=[
            pl.BlockSpec((1, n), lambda g: (0, 0)),
            pl.BlockSpec((n, width // groups), lambda g: (0, g)),
        ],
        out_specs=[
            pl.BlockSpec((1, n, KEY_CHUNK), lambda g: (g, 0, 0)),
            pl.BlockSpec((1, n, QUERY_WIDTH), lambda g: (g, 0, 0)),
        ],
        out_shape=[
            jax.ShapeDtypeStruct((groups, n, KEY_CHUNK), rows.dtype),
            jax.ShapeDtypeStruct((groups, n, QUERY_WIDTH), rows.dtype),
        ],
        compiler_params=params(),
        cost_estimate=cost(0, 2 * rows.size * 2),
        name="split_rows",
    )(target.reshape(1, n), rows)


def sort_kernel(per_pair, chunk_ref, keys_ref, forward_ref, backward_ref):
    n = chunk_ref.shape[0]
    parts, padded, _ = keys_ref.shape
    coded = chunk_ref[:, KV_WIDTH:].astype(jnp.float32)
    column = coded[:, 0:1] * 256.0 + coded[:, 1:2]
    row = column_to_row(column)
    rank_row = jnp.sum(jnp.where(column < row, 1.0, 0.0), axis=0, keepdims=True)
    rank_column = jnp.sum(jnp.where(row < column, 1.0, 0.0), axis=1, keepdims=True)
    down = iota((n, n), 0).astype(jnp.float32)
    across = iota((n, n), 1).astype(jnp.float32)
    forward_ref[...] = jnp.where(rank_row == down, 1.0, 0.0).astype(jnp.bfloat16)
    backward_ref[...] = jnp.where(rank_column == across, 1.0, 0.0).astype(jnp.bfloat16)
    local = jnp.where(coded[:, 0:1] - 2.0 * jnp.floor(coded[:, 0:1] * 0.5) > 0.5, 0.0, -256.0)
    local = local + coded[:, 1:2]
    tile = jnp.where(iota((n, LANES), 1) == 0, local, 0.0).astype(jnp.bfloat16)
    wanted = jnp.concatenate(
        [(iota((padded, n), 0) + (p * (n // parts) - per_pair)) & (n - 1) for p in range(parts)],
        axis=0,
    ).astype(jnp.float32)
    order = jnp.where(rank_row == wanted, 1.0, 0.0).astype(jnp.bfloat16)
    keys = jnp.dot(order, chunk_ref[:, :KV_WIDTH], preferred_element_type=jnp.float32)
    places = jnp.dot(order, tile, preferred_element_type=jnp.float32)
    for p in range(parts):
        rows = slice(p * padded, (p + 1) * padded)
        keys_ref[p, :, :KV_WIDTH] = keys[rows].astype(keys_ref.dtype)
        keys_ref[p, :, KV_WIDTH:] = places[rows].astype(keys_ref.dtype)


def sort_rows(chunk, parts, per_pair):
    n = chunk.shape[0]
    padded = n // parts + per_pair
    return pl.pallas_call(
        functools.partial(sort_kernel, per_pair),
        in_specs=whole(1),
        out_specs=whole(3),
        out_shape=[
            jax.ShapeDtypeStruct((parts, padded, KEY_CHUNK), chunk.dtype),
            jax.ShapeDtypeStruct((n, n), jnp.bfloat16),
            jax.ShapeDtypeStruct((n, n), jnp.bfloat16),
        ],
        compiler_params=params(),
        cost_estimate=cost(2 * n * chunk.size, 4 * chunk.size),
        name="sort_rows",
    )(chunk)


def permute_kernel(order_ref, chunk_ref, out_ref):
    out_ref[...] = jnp.dot(
        order_ref[...], chunk_ref[...], preferred_element_type=jnp.float32
    ).astype(out_ref.dtype)


def permute_rows(order, chunk, name):
    return pl.pallas_call(
        permute_kernel,
        in_specs=whole(2),
        out_specs=pl.BlockSpec(memory_space=pltpu.VMEM),
        out_shape=jax.ShapeDtypeStruct(chunk.shape, chunk.dtype),
        compiler_params=params(),
        cost_estimate=cost(2 * chunk.shape[0] * chunk.size, 4 * chunk.size),
        name=name,
    )(order, chunk)


def arrange_kernel(per_pair, got_ref, load_ref, place_ref):
    sources, padded, _ = got_ref.shape
    blocks = padded // per_pair
    span = sources * per_pair
    pieces = [got_ref[s].astype(jnp.float32) for s in range(sources)]
    places = []
    for b in range(blocks):
        rows = slice(b * per_pair, (b + 1) * per_pair)
        block = jnp.concatenate([piece[rows] for piece in pieces], axis=0)
        load_ref[b * span : (b + 1) * span, :] = block[:, :KV_WIDTH].astype(load_ref.dtype)
        places.append(block[:, KV_WIDTH:])
        place_ref[b * span : (b + 1) * span, :] = places[b]
    rows = jnp.zeros((16, LANES), jnp.float32)
    for b in range(1, blocks):
        pair = jnp.concatenate([places[b - 1], places[b]], axis=0)[:, 0:1]
        rows = jnp.where(iota((16, LANES), 0) == b - 1, column_to_row(pair), rows)
    load_ref[blocks * span :, :LANES] = rows.astype(load_ref.dtype)
    load_ref[blocks * span :, LANES:] = jnp.zeros((16, LANES), load_ref.dtype)


def arrange(got, per_pair):
    sources, padded, _ = got.shape
    rows = sources * padded
    return pl.pallas_call(
        functools.partial(arrange_kernel, per_pair),
        in_specs=whole(1),
        out_specs=whole(2),
        out_shape=[
            jax.ShapeDtypeStruct((rows + 16, KV_WIDTH), got.dtype),
            jax.ShapeDtypeStruct((rows, LANES), jnp.float32),
        ],
        compiler_params=params(),
        cost_estimate=cost(0, 4 * got.size),
        name="arrange",
    )(got)


def attend_kernel(per_pair, loads, starts_ref, place_ref, query_ref, *refs):
    load_refs, (out_ref, key_ref, value_ref, done_ref) = refs[:loads], refs[loads:]
    sources = out_ref.shape[0]
    span = sources * per_pair
    blocks = out_ref.shape[1] // per_pair
    pair = 2 * span
    scale = math.log2(math.e) / math.sqrt(HEAD_SIZE)
    half = float(BLOCK // 2)
    lane = iota((1, pair), 1)
    shift = jnp.where(lane < span, half - BLOCK, half)
    starts = starts_ref[...]
    for b in range(blocks):
        rows = slice(b * span, b * span + pair)
        for at, load_ref in enumerate(load_refs):
            key_ref[at * pair : (at + 1) * pair, :] = load_ref[rows, :HEAD_SIZE]
            value_ref[at * pair : (at + 1) * pair, :] = load_ref[rows, HEAD_SIZE:]
        key_place = jnp.concatenate(
            [
                load_ref[(blocks + 1) * span :, :LANES].astype(jnp.float32)[b : b + 1] + shift
                for load_ref in load_refs
            ],
            axis=1,
        )
        place = place_ref[(b + 1) * span : (b + 2) * span, 0:1] + half
        base = float(b * BLOCK)
        start = jnp.max(
            jnp.where(starts <= place + base, starts, -1e9), axis=1, keepdims=True
        )
        allowed = (key_place >= start - base) & (key_place <= place)
        bias = jnp.where(allowed, 0.0, MASKED)
        query = query_ref[b * span : (b + 1) * span, :]
        query = jnp.concatenate(
            [query[:, h * HEAD_SIZE : (h + 1) * HEAD_SIZE] for h in range(QUERY_PER_KEY)], axis=0
        )
        scores = lax.dot_general(
            query, key_ref[...], (((1,), (1,)), ((), ())), preferred_element_type=jnp.float32
        )
        scores = scores.reshape(QUERY_PER_KEY, span, loads * pair) * scale + bias[None]
        weights = jnp.exp2(scores - jnp.max(scores, axis=2, keepdims=True))
        total = jnp.sum(weights, axis=2, keepdims=True).reshape(QUERY_PER_KEY * span, 1)
        weights = weights.astype(jnp.bfloat16).reshape(QUERY_PER_KEY * span, loads * pair)
        done = jnp.dot(weights, value_ref[...], preferred_element_type=jnp.float32) / total
        for h in range(QUERY_PER_KEY):
            for s in range(sources):
                first = h * span + s * per_pair
                done_ref[
                    s, b * per_pair : (b + 1) * per_pair, h * HEAD_SIZE : (h + 1) * HEAD_SIZE
                ] = done[first : first + per_pair]
    out_ref[...] = done_ref[...].astype(out_ref.dtype)


def attend(starts, places, queries, loads, sources, per_pair):
    n = queries.shape[0]
    keys = len(loads) * 2 * sources * per_pair
    shape = (sources, n // sources, QUERY_WIDTH)
    return pl.pallas_call(
        functools.partial(attend_kernel, per_pair, len(loads)),
        in_specs=whole(3 + len(loads)),
        out_specs=pl.BlockSpec(memory_space=pltpu.VMEM),
        out_shape=jax.ShapeDtypeStruct(shape, queries.dtype),
        scratch_shapes=[
            pltpu.VMEM((keys, HEAD_SIZE), queries.dtype),
            pltpu.VMEM((keys, HEAD_SIZE), queries.dtype),
            pltpu.VMEM(shape, jnp.float32),
        ],
        compiler_params=params(),
        cost_estimate=cost(4 * n * keys * QUERY_WIDTH, 4 * n * QUERY_WIDTH),
        name="attend",
    )(starts, places, queries, *loads)


def exchange(blocks, axis):
    return lax.all_to_all(blocks, axis, split_axis=0, concat_axis=0, tiled=True)


def per_device(section_token_rows, row_target, doc_lengths):
    tp_count = lax.axis_size("tp")
    slabs = lax.axis_size("zh")
    parts = lax.axis_size("x") * lax.axis_size("zl")
    local_rows = section_token_rows.shape[0]
    tok_dev = local_rows * tp_count
    per_pair = tok_dev // (parts * slabs)
    part = lax.axis_index("x") * lax.axis_size("zl") + lax.axis_index("zl")
    starts = (jnp.cumsum(doc_lengths) - doc_lengths - part * (slabs * tok_dev)).reshape(1, -1)
    starts = starts.astype(jnp.float32)

    keys, queries = split_rows(section_token_rows, row_target, tp_count)
    keys = exchange(keys, "tp").reshape(tok_dev, KEY_CHUNK)
    keys, forward, backward = sort_rows(keys, parts, per_pair)
    got = exchange(keys, PART)
    got, queries = lax.optimization_barrier((got, queries))
    load, places = arrange(got, per_pair)

    queries = exchange(queries, "tp").reshape(tok_dev, QUERY_WIDTH)
    queries = permute_rows(forward, queries, "sort_queries")
    queries = exchange(queries.reshape(parts, tok_dev // parts, QUERY_WIDTH), PART)
    queries = queries.reshape(parts, slabs, per_pair, QUERY_WIDTH).transpose(1, 0, 2, 3)
    queries = queries.reshape(tok_dev, QUERY_WIDTH)

    route = []
    for at in range(slabs):
        for low in range(2):
            to = (at + 1 - 2 * low) % slabs
            route.append((at * 2 + low, to * 2 + low))
    loads = [load]
    for _ in range(slabs - 1):
        loads.append(lax.ppermute(loads[-1], RING, route))

    done = attend(starts, places, queries, loads, parts, per_pair)
    back = exchange(done, PART).reshape(tok_dev, QUERY_WIDTH)
    back = permute_rows(backward, back, "unsort").reshape(tp_count, local_rows, QUERY_WIDTH)
    back = exchange(back, "tp")
    return back.transpose(1, 0, 2).reshape(local_rows, tp_count * QUERY_WIDTH)


def solution(mesh):
    shape = (4, 8, 2, mesh.shape["tp"])
    ring_mesh = Mesh(mesh.devices.reshape(shape), AXES)
    placed = (P(AXES, None), P(AXES), P())
    return jax.shard_map(
        per_device, mesh=ring_mesh, in_specs=placed, out_specs=P(AXES, None), check_vma=False
    )
```

```python
import functools
import math

import jax
import jax.numpy as jnp
from jax import lax
from jax.experimental import pallas as pl
from jax.experimental.pallas import tpu as pltpu
from jax.sharding import Mesh
from jax.sharding import PartitionSpec as P

HEAD_SIZE = 128
QUERY_PER_KEY = 5
LANES = 128
BLOCK = 512
QUERY_WIDTH = QUERY_PER_KEY * HEAD_SIZE
KV_WIDTH = 2 * HEAD_SIZE
KEY_CHUNK = KV_WIDTH + LANES
MASKED = -1e30
VMEM_LIMIT = 24 * 1024 * 1024
AXES = ("x", "zh", "zl", "tp")
PART = ("x", "zl")
RING = ("zh", "zl")
MEETINGS = (3, 6)


def whole(n):
    return [pl.BlockSpec(memory_space=pltpu.VMEM)] * n


def params():
    return pltpu.CompilerParams(vmem_limit_bytes=VMEM_LIMIT)


def cost(flops, moved):
    return pl.CostEstimate(flops=flops, bytes_accessed=moved, transcendentals=0)


def iota(shape, axis):
    return lax.broadcasted_iota(jnp.int32, shape, axis)


def eye(n):
    return iota((n, n), 0) == iota((n, n), 1)


def column_to_row(column):
    n = column.shape[0]
    return jnp.sum(jnp.where(eye(n), column, 0.0), axis=0, keepdims=True)


def split_kernel(target_ref, rows_ref, keys_ref, queries_ref):
    n = rows_ref.shape[0]
    target = jnp.sum(jnp.where(eye(n), target_ref[...], 0), axis=1, keepdims=True)
    lane = iota((n, LANES), 1)
    coded = jnp.where(lane == 0, target >> 8, jnp.where(lane == 1, target & 255, 0))
    queries_ref[0] = rows_ref[:, :QUERY_WIDTH]
    keys_ref[0, :, :KV_WIDTH] = rows_ref[:, QUERY_WIDTH:]
    keys_ref[0, :, KV_WIDTH:] = coded.astype(jnp.float32).astype(jnp.bfloat16)


def split_rows(rows, target, groups):
    n, width = rows.shape
    return pl.pallas_call(
        split_kernel,
        grid=(groups,),
        in_specs=[
            pl.BlockSpec((1, n), lambda g: (0, 0)),
            pl.BlockSpec((n, width // groups), lambda g: (0, g)),
        ],
        out_specs=[
            pl.BlockSpec((1, n, KEY_CHUNK), lambda g: (g, 0, 0)),
            pl.BlockSpec((1, n, QUERY_WIDTH), lambda g: (g, 0, 0)),
        ],
        out_shape=[
            jax.ShapeDtypeStruct((groups, n, KEY_CHUNK), rows.dtype),
            jax.ShapeDtypeStruct((groups, n, QUERY_WIDTH), rows.dtype),
        ],
        compiler_params=params(),
        cost_estimate=cost(0, 2 * rows.size * 2),
        name="split_rows",
    )(target.reshape(1, n), rows)


def sort_kernel(per_pair, chunk_ref, keys_ref, forward_ref, backward_ref):
    n = chunk_ref.shape[0]
    parts, padded, _ = keys_ref.shape
    coded = chunk_ref[:, KV_WIDTH:].astype(jnp.float32)
    column = coded[:, 0:1] * 256.0 + coded[:, 1:2]
    row = column_to_row(column)
    rank_row = jnp.sum(jnp.where(column < row, 1.0, 0.0), axis=0, keepdims=True)
    rank_column = jnp.sum(jnp.where(row < column, 1.0, 0.0), axis=1, keepdims=True)
    down = iota((n, n), 0).astype(jnp.float32)
    across = iota((n, n), 1).astype(jnp.float32)
    forward_ref[...] = jnp.where(rank_row == down, 1.0, 0.0).astype(jnp.bfloat16)
    backward_ref[...] = jnp.where(rank_column == across, 1.0, 0.0).astype(jnp.bfloat16)
    local = jnp.where(coded[:, 0:1] - 2.0 * jnp.floor(coded[:, 0:1] * 0.5) > 0.5, 0.0, -256.0)
    local = local + coded[:, 1:2]
    tile = jnp.where(iota((n, LANES), 1) == 0, local, 0.0).astype(jnp.bfloat16)
    wanted = jnp.concatenate(
        [(iota((padded, n), 0) + (p * (n // parts) - per_pair)) & (n - 1) for p in range(parts)],
        axis=0,
    ).astype(jnp.float32)
    order = jnp.where(rank_row == wanted, 1.0, 0.0).astype(jnp.bfloat16)
    keys = jnp.dot(order, chunk_ref[:, :KV_WIDTH], preferred_element_type=jnp.float32)
    places = jnp.dot(order, tile, preferred_element_type=jnp.float32)
    for p in range(parts):
        rows = slice(p * padded, (p + 1) * padded)
        keys_ref[p, :, :KV_WIDTH] = keys[rows].astype(keys_ref.dtype)
        keys_ref[p, :, KV_WIDTH:] = places[rows].astype(keys_ref.dtype)


def sort_rows(chunk, parts, per_pair):
    n = chunk.shape[0]
    padded = n // parts + per_pair
    return pl.pallas_call(
        functools.partial(sort_kernel, per_pair),
        in_specs=whole(1),
        out_specs=whole(3),
        out_shape=[
            jax.ShapeDtypeStruct((parts, padded, KEY_CHUNK), chunk.dtype),
            jax.ShapeDtypeStruct((n, n), jnp.bfloat16),
            jax.ShapeDtypeStruct((n, n), jnp.bfloat16),
        ],
        compiler_params=params(),
        cost_estimate=cost(2 * n * chunk.size, 4 * chunk.size),
        name="sort_rows",
    )(chunk)


def permute_kernel(order_ref, chunk_ref, out_ref):
    out_ref[...] = jnp.dot(
        order_ref[...], chunk_ref[...], preferred_element_type=jnp.float32
    ).astype(out_ref.dtype)


def permute_rows(order, chunk, name):
    return pl.pallas_call(
        permute_kernel,
        in_specs=whole(2),
        out_specs=pl.BlockSpec(memory_space=pltpu.VMEM),
        out_shape=jax.ShapeDtypeStruct(chunk.shape, chunk.dtype),
        compiler_params=params(),
        cost_estimate=cost(2 * chunk.shape[0] * chunk.size, 4 * chunk.size),
        name=name,
    )(order, chunk)


def arrange_kernel(per_pair, got_ref, key_ref, value_ref, place_ref):
    sources, padded, _ = got_ref.shape
    blocks = padded // per_pair
    span = sources * per_pair
    pieces = [got_ref[s].astype(jnp.float32) for s in range(sources)]
    places = []
    for b in range(blocks):
        rows = slice(b * per_pair, (b + 1) * per_pair)
        block = jnp.concatenate([piece[rows] for piece in pieces], axis=0)
        at = slice(b * span, (b + 1) * span)
        key_ref[at, :] = block[:, :HEAD_SIZE].astype(key_ref.dtype)
        value_ref[at, :] = block[:, HEAD_SIZE:KV_WIDTH].astype(value_ref.dtype)
        places.append(block[:, KV_WIDTH:])
        place_ref[at, :] = places[b]
    rows = jnp.zeros((16, LANES), jnp.float32)
    for b in range(1, blocks):
        pair = jnp.concatenate([places[b - 1], places[b]], axis=0)[:, 0:1]
        rows = jnp.where(iota((16, LANES), 0) == b - 1, column_to_row(pair), rows)
    key_ref[blocks * span :, :] = rows.astype(key_ref.dtype)


def arrange(got, per_pair):
    sources, padded, _ = got.shape
    rows = sources * padded
    return pl.pallas_call(
        functools.partial(arrange_kernel, per_pair),
        in_specs=whole(1),
        out_specs=whole(3),
        out_shape=[
            jax.ShapeDtypeStruct((rows + 16, HEAD_SIZE), got.dtype),
            jax.ShapeDtypeStruct((rows, HEAD_SIZE), got.dtype),
            jax.ShapeDtypeStruct((rows, LANES), jnp.float32),
        ],
        compiler_params=params(),
        cost_estimate=cost(0, 4 * got.size),
        name="arrange",
    )(got)


def attend_kernel(per_pair, loads, starts_ref, place_ref, query_ref, *refs):
    load_refs, value_refs = refs[:loads], refs[loads : 2 * loads]
    out_ref, key_ref, value_ref, done_ref = refs[2 * loads :]
    sources = out_ref.shape[0]
    span = sources * per_pair
    blocks = out_ref.shape[1] // per_pair
    pair = 2 * span
    scale = math.log2(math.e) / math.sqrt(HEAD_SIZE)
    half = float(BLOCK // 2)
    lane = iota((1, pair), 1)
    shift = jnp.where(lane < span, half - BLOCK, half)
    starts = starts_ref[...]
    for b in range(blocks):
        rows = slice(b * span, b * span + pair)
        for at in range(loads):
            key_ref[at * pair : (at + 1) * pair, :] = load_refs[at][rows, :]
            value_ref[at * pair : (at + 1) * pair, :] = value_refs[at][rows, :]
        key_place = jnp.concatenate(
            [
                load_ref[(blocks + 1) * span :, :].astype(jnp.float32)[b : b + 1] + shift
                for load_ref in load_refs
            ],
            axis=1,
        )
        place = place_ref[(b + 1) * span : (b + 2) * span, 0:1] + half
        base = float(b * BLOCK)
        start = jnp.max(
            jnp.where(starts <= place + base, starts, -1e9), axis=1, keepdims=True
        )
        allowed = (key_place >= start - base) & (key_place <= place)
        bias = jnp.where(allowed, 0.0, MASKED)
        query = query_ref[b * span : (b + 1) * span, :]
        query = jnp.concatenate(
            [query[:, h * HEAD_SIZE : (h + 1) * HEAD_SIZE] for h in range(QUERY_PER_KEY)], axis=0
        )
        scores = lax.dot_general(
            query, key_ref[...], (((1,), (1,)), ((), ())), preferred_element_type=jnp.float32
        )
        scores = scores.reshape(QUERY_PER_KEY, span, loads * pair) * scale + bias[None]
        weights = jnp.exp2(scores - jnp.max(scores, axis=2, keepdims=True))
        total = jnp.sum(weights, axis=2, keepdims=True).reshape(QUERY_PER_KEY * span, 1)
        weights = weights.astype(jnp.bfloat16).reshape(QUERY_PER_KEY * span, loads * pair)
        done = jnp.dot(weights, value_ref[...], preferred_element_type=jnp.float32) / total
        for h in range(QUERY_PER_KEY):
            for s in range(sources):
                first = h * span + s * per_pair
                done_ref[
                    s, b * per_pair : (b + 1) * per_pair, h * HEAD_SIZE : (h + 1) * HEAD_SIZE
                ] = done[first : first + per_pair]
    out_ref[...] = done_ref[...].astype(out_ref.dtype)


def attend(starts, places, queries, loads, values, sources, per_pair):
    n = queries.shape[0]
    keys = len(loads) * 2 * sources * per_pair
    shape = (sources, n // sources, QUERY_WIDTH)
    return pl.pallas_call(
        functools.partial(attend_kernel, per_pair, len(loads)),
        in_specs=whole(3 + 2 * len(loads)),
        out_specs=pl.BlockSpec(memory_space=pltpu.VMEM),
        out_shape=jax.ShapeDtypeStruct(shape, queries.dtype),
        scratch_shapes=[
            pltpu.VMEM((keys, HEAD_SIZE), queries.dtype),
            pltpu.VMEM((keys, HEAD_SIZE), queries.dtype),
            pltpu.VMEM(shape, jnp.float32),
        ],
        compiler_params=params(),
        cost_estimate=cost(4 * n * keys * QUERY_WIDTH, 4 * n * QUERY_WIDTH),
        name="attend",
    )(starts, places, queries, *loads, *values)


def exchange(blocks, axis):
    return lax.all_to_all(blocks, axis, split_axis=0, concat_axis=0, tiled=True)


def per_device(section_token_rows, row_target, doc_lengths):
    tp_count = lax.axis_size("tp")
    slabs = lax.axis_size("zh")
    parts = lax.axis_size("x") * lax.axis_size("zl")
    local_rows = section_token_rows.shape[0]
    tok_dev = local_rows * tp_count
    per_pair = tok_dev // (parts * slabs)
    part = lax.axis_index("x") * lax.axis_size("zl") + lax.axis_index("zl")
    starts = (jnp.cumsum(doc_lengths) - doc_lengths - part * (slabs * tok_dev)).reshape(1, -1)
    starts = starts.astype(jnp.float32)

    keys, queries = split_rows(section_token_rows, row_target, tp_count)
    keys = exchange(keys, "tp").reshape(tok_dev, KEY_CHUNK)
    keys, forward, backward = sort_rows(keys, parts, per_pair)
    load, value, places = arrange(exchange(keys, PART), per_pair)
    load, value, queries = lax.optimization_barrier((load, value, queries))

    route = []
    for at in range(slabs):
        for low in range(2):
            to = (at + 1 - 2 * low) % slabs
            route.append((at * 2 + low, to * 2 + low))
    loads, values = [load], [value]
    queries = exchange(queries, "tp").reshape(tok_dev, QUERY_WIDTH)
    for step in range(1, slabs):
        loads.append(lax.ppermute(loads[-1], RING, route))
        values.append(lax.ppermute(values[-1], RING, route))
        if step in MEETINGS:
            loads[-1], values[-1], queries = lax.optimization_barrier(
                (loads[-1], values[-1], queries)
            )
        if step == MEETINGS[0]:
            queries = permute_rows(forward, queries, "sort_queries")
            queries = exchange(queries.reshape(parts, tok_dev // parts, QUERY_WIDTH), PART)
    queries = queries.reshape(parts, slabs, per_pair, QUERY_WIDTH).transpose(1, 0, 2, 3)
    queries = queries.reshape(tok_dev, QUERY_WIDTH)

    done = attend(starts, places, queries, loads, values, parts, per_pair)
    back = exchange(done, PART).reshape(tok_dev, QUERY_WIDTH)
    back = permute_rows(backward, back, "unsort").reshape(tp_count, local_rows, QUERY_WIDTH)
    back = exchange(back, "tp")
    return back.transpose(1, 0, 2).reshape(local_rows, tp_count * QUERY_WIDTH)


def solution(mesh):
    shape = (4, 8, 2, mesh.shape["tp"])
    ring_mesh = Mesh(mesh.devices.reshape(shape), AXES)
    placed = (P(AXES, None), P(AXES), P())
    return jax.shard_map(
        per_device, mesh=ring_mesh, in_specs=placed, out_specs=P(AXES, None), check_vma=False
    )
```

```python
import functools
import math

import jax
import jax.numpy as jnp
from jax import lax
from jax.experimental import pallas as pl
from jax.experimental.pallas import tpu as pltpu
from jax.sharding import Mesh
from jax.sharding import PartitionSpec as P

HEAD_SIZE = 128
QUERY_PER_KEY = 5
LANES = 128
BLOCK = 512
QUERY_WIDTH = QUERY_PER_KEY * HEAD_SIZE
KV_WIDTH = 2 * HEAD_SIZE
KEY_CHUNK = KV_WIDTH + LANES
MASKED = -1e30
VMEM_LIMIT = 24 * 1024 * 1024
AXES = ("x", "zh", "zl", "tp")
PART = ("x", "zl")
RING = ("zh", "zl")
MEETINGS = (1, 3)


def whole(n):
    return [pl.BlockSpec(memory_space=pltpu.VMEM)] * n


def params():
    return pltpu.CompilerParams(vmem_limit_bytes=VMEM_LIMIT)


def cost(flops, moved):
    return pl.CostEstimate(flops=flops, bytes_accessed=moved, transcendentals=0)


def iota(shape, axis):
    return lax.broadcasted_iota(jnp.int32, shape, axis)


def eye(n):
    return iota((n, n), 0) == iota((n, n), 1)


def column_to_row(column):
    n = column.shape[0]
    return jnp.sum(jnp.where(eye(n), column, 0.0), axis=0, keepdims=True)


def split_keys_kernel(target_ref, key_ref, value_ref, out_ref):
    n = key_ref.shape[0]
    target = jnp.sum(jnp.where(eye(n), target_ref[...], 0), axis=1, keepdims=True)
    lane = iota((n, LANES), 1)
    coded = jnp.where(lane == 0, target >> 8, jnp.where(lane == 1, target & 255, 0))
    out_ref[0, :, :HEAD_SIZE] = key_ref[...]
    out_ref[0, :, HEAD_SIZE:KV_WIDTH] = value_ref[...]
    out_ref[0, :, KV_WIDTH:] = coded.astype(jnp.float32).astype(jnp.bfloat16)


def split_keys(rows, target, groups):
    n = rows.shape[0]
    heads = QUERY_PER_KEY + 2
    return pl.pallas_call(
        split_keys_kernel,
        grid=(groups,),
        in_specs=[
            pl.BlockSpec((1, n), lambda g: (0, 0)),
            pl.BlockSpec((n, HEAD_SIZE), lambda g: (0, heads * g + QUERY_PER_KEY)),
            pl.BlockSpec((n, HEAD_SIZE), lambda g: (0, heads * g + QUERY_PER_KEY + 1)),
        ],
        out_specs=pl.BlockSpec((1, n, KEY_CHUNK), lambda g: (g, 0, 0)),
        out_shape=jax.ShapeDtypeStruct((groups, n, KEY_CHUNK), rows.dtype),
        compiler_params=params(),
        cost_estimate=cost(0, 4 * groups * n * KEY_CHUNK),
        name="split_keys",
    )(target.reshape(1, n), rows, rows)


def split_queries_kernel(rows_ref, out_ref):
    out_ref[0] = rows_ref[:, :QUERY_WIDTH]


def split_queries(rows, groups):
    n, width = rows.shape
    return pl.pallas_call(
        split_queries_kernel,
        grid=(groups,),
        in_specs=[pl.BlockSpec((n, width // groups), lambda g: (0, g))],
        out_specs=pl.BlockSpec((1, n, QUERY_WIDTH), lambda g: (g, 0, 0)),
        out_shape=jax.ShapeDtypeStruct((groups, n, QUERY_WIDTH), rows.dtype),
        compiler_params=params(),
        cost_estimate=cost(0, 4 * rows.size),
        name="split_queries",
    )(rows)


def sort_kernel(per_pair, chunk_ref, keys_ref, forward_ref, backward_ref):
    n = chunk_ref.shape[0]
    parts, padded, _ = keys_ref.shape
    coded = chunk_ref[:, KV_WIDTH:].astype(jnp.float32)
    column = coded[:, 0:1] * 256.0 + coded[:, 1:2]
    row = column_to_row(column)
    rank_row = jnp.sum(jnp.where(column < row, 1.0, 0.0), axis=0, keepdims=True)
    rank_column = jnp.sum(jnp.where(row < column, 1.0, 0.0), axis=1, keepdims=True)
    down = iota((n, n), 0).astype(jnp.float32)
    across = iota((n, n), 1).astype(jnp.float32)
    forward_ref[...] = jnp.where(rank_row == down, 1.0, 0.0).astype(jnp.bfloat16)
    backward_ref[...] = jnp.where(rank_column == across, 1.0, 0.0).astype(jnp.bfloat16)
    local = jnp.where(coded[:, 0:1] - 2.0 * jnp.floor(coded[:, 0:1] * 0.5) > 0.5, 0.0, -256.0)
    local = local + coded[:, 1:2]
    tile = jnp.where(iota((n, LANES), 1) == 0, local, 0.0).astype(jnp.bfloat16)
    wanted = jnp.concatenate(
        [(iota((padded, n), 0) + (p * (n // parts) - per_pair)) & (n - 1) for p in range(parts)],
        axis=0,
    ).astype(jnp.float32)
    order = jnp.where(rank_row == wanted, 1.0, 0.0).astype(jnp.bfloat16)
    keys = jnp.dot(order, chunk_ref[:, :KV_WIDTH], preferred_element_type=jnp.float32)
    places = jnp.dot(order, tile, preferred_element_type=jnp.float32)
    for p in range(parts):
        rows = slice(p * padded, (p + 1) * padded)
        keys_ref[p, :, :KV_WIDTH] = keys[rows].astype(keys_ref.dtype)
        keys_ref[p, :, KV_WIDTH:] = places[rows].astype(keys_ref.dtype)


def sort_rows(chunk, parts, per_pair):
    n = chunk.shape[0]
    padded = n // parts + per_pair
    return pl.pallas_call(
        functools.partial(sort_kernel, per_pair),
        in_specs=whole(1),
        out_specs=whole(3),
        out_shape=[
            jax.ShapeDtypeStruct((parts, padded, KEY_CHUNK), chunk.dtype),
            jax.ShapeDtypeStruct((n, n), jnp.bfloat16),
            jax.ShapeDtypeStruct((n, n), jnp.bfloat16),
        ],
        compiler_params=params(),
        cost_estimate=cost(2 * n * chunk.size, 4 * chunk.size),
        name="sort_rows",
    )(chunk)


def permute_kernel(order_ref, chunk_ref, out_ref):
    out_ref[...] = jnp.dot(
        order_ref[...], chunk_ref[...], preferred_element_type=jnp.float32
    ).astype(out_ref.dtype)


def permute_rows(order, chunk, name):
    return pl.pallas_call(
        permute_kernel,
        in_specs=whole(2),
        out_specs=pl.BlockSpec(memory_space=pltpu.VMEM),
        out_shape=jax.ShapeDtypeStruct(chunk.shape, chunk.dtype),
        compiler_params=params(),
        cost_estimate=cost(2 * chunk.shape[0] * chunk.size, 4 * chunk.size),
        name=name,
    )(order, chunk)


def arrange_kernel(per_pair, got_ref, key_ref, value_ref, place_ref):
    sources, padded, _ = got_ref.shape
    blocks = padded // per_pair
    span = sources * per_pair
    pieces = [got_ref[s].astype(jnp.float32) for s in range(sources)]
    places = []
    for b in range(blocks):
        rows = slice(b * per_pair, (b + 1) * per_pair)
        block = jnp.concatenate([piece[rows] for piece in pieces], axis=0)
        at = slice(b * span, (b + 1) * span)
        key_ref[at, :] = block[:, :HEAD_SIZE].astype(key_ref.dtype)
        value_ref[at, :] = block[:, HEAD_SIZE:KV_WIDTH].astype(value_ref.dtype)
        places.append(block[:, KV_WIDTH:])
        place_ref[at, :] = places[b]
    rows = jnp.zeros((16, LANES), jnp.float32)
    for b in range(1, blocks):
        pair = jnp.concatenate([places[b - 1], places[b]], axis=0)[:, 0:1]
        rows = jnp.where(iota((16, LANES), 0) == b - 1, column_to_row(pair), rows)
    key_ref[blocks * span :, :] = rows.astype(key_ref.dtype)


def arrange(got, per_pair):
    sources, padded, _ = got.shape
    rows = sources * padded
    return pl.pallas_call(
        functools.partial(arrange_kernel, per_pair),
        in_specs=whole(1),
        out_specs=whole(3),
        out_shape=[
            jax.ShapeDtypeStruct((rows + 16, HEAD_SIZE), got.dtype),
            jax.ShapeDtypeStruct((rows, HEAD_SIZE), got.dtype),
            jax.ShapeDtypeStruct((rows, LANES), jnp.float32),
        ],
        compiler_params=params(),
        cost_estimate=cost(0, 4 * got.size),
        name="arrange",
    )(got)


def attend_kernel(per_pair, loads, starts_ref, place_ref, query_ref, *refs):
    load_refs, value_refs = refs[:loads], refs[loads : 2 * loads]
    out_ref, key_ref, value_ref, done_ref = refs[2 * loads :]
    sources = out_ref.shape[0]
    span = sources * per_pair
    blocks = out_ref.shape[1] // per_pair
    pair = 2 * span
    scale = math.log2(math.e) / math.sqrt(HEAD_SIZE)
    half = float(BLOCK // 2)
    lane = iota((1, pair), 1)
    shift = jnp.where(lane < span, half - BLOCK, half)
    starts = starts_ref[...]
    for b in range(blocks):
        rows = slice(b * span, b * span + pair)
        for at in range(loads):
            key_ref[at * pair : (at + 1) * pair, :] = load_refs[at][rows, :]
            value_ref[at * pair : (at + 1) * pair, :] = value_refs[at][rows, :]
        key_place = jnp.concatenate(
            [
                load_ref[(blocks + 1) * span :, :].astype(jnp.float32)[b : b + 1] + shift
                for load_ref in load_refs
            ],
            axis=1,
        )
        place = place_ref[(b + 1) * span : (b + 2) * span, 0:1] + half
        base = float(b * BLOCK)
        start = jnp.max(
            jnp.where(starts <= place + base, starts, -1e9), axis=1, keepdims=True
        )
        allowed = (key_place >= start - base) & (key_place <= place)
        bias = jnp.where(allowed, 0.0, MASKED)
        query = query_ref[b * span : (b + 1) * span, :]
        query = jnp.concatenate(
            [query[:, h * HEAD_SIZE : (h + 1) * HEAD_SIZE] for h in range(QUERY_PER_KEY)], axis=0
        )
        scores = lax.dot_general(
            query, key_ref[...], (((1,), (1,)), ((), ())), preferred_element_type=jnp.float32
        )
        scores = scores.reshape(QUERY_PER_KEY, span, loads * pair) * scale + bias[None]
        weights = jnp.exp2(scores - jnp.max(scores, axis=2, keepdims=True))
        total = jnp.sum(weights, axis=2, keepdims=True).reshape(QUERY_PER_KEY * span, 1)
        weights = weights.astype(jnp.bfloat16).reshape(QUERY_PER_KEY * span, loads * pair)
        done = jnp.dot(weights, value_ref[...], preferred_element_type=jnp.float32) / total
        for h in range(QUERY_PER_KEY):
            for s in range(sources):
                first = h * span + s * per_pair
                done_ref[
                    s, b * per_pair : (b + 1) * per_pair, h * HEAD_SIZE : (h + 1) * HEAD_SIZE
                ] = done[first : first + per_pair]
    out_ref[...] = done_ref[...].astype(out_ref.dtype)


def attend(starts, places, queries, loads, values, sources, per_pair):
    n = queries.shape[0]
    keys = len(loads) * 2 * sources * per_pair
    shape = (sources, n // sources, QUERY_WIDTH)
    return pl.pallas_call(
        functools.partial(attend_kernel, per_pair, len(loads)),
        in_specs=whole(3 + 2 * len(loads)),
        out_specs=pl.BlockSpec(memory_space=pltpu.VMEM),
        out_shape=jax.ShapeDtypeStruct(shape, queries.dtype),
        scratch_shapes=[
            pltpu.VMEM((keys, HEAD_SIZE), queries.dtype),
            pltpu.VMEM((keys, HEAD_SIZE), queries.dtype),
            pltpu.VMEM(shape, jnp.float32),
        ],
        compiler_params=params(),
        cost_estimate=cost(4 * n * keys * QUERY_WIDTH, 4 * n * QUERY_WIDTH),
        name="attend",
    )(starts, places, queries, *loads, *values)


def exchange(blocks, axis):
    return lax.all_to_all(blocks, axis, split_axis=0, concat_axis=0, tiled=True)


def per_device(section_token_rows, row_target, doc_lengths):
    tp_count = lax.axis_size("tp")
    slabs = lax.axis_size("zh")
    parts = lax.axis_size("x") * lax.axis_size("zl")
    local_rows = section_token_rows.shape[0]
    tok_dev = local_rows * tp_count
    per_pair = tok_dev // (parts * slabs)
    part = lax.axis_index("x") * lax.axis_size("zl") + lax.axis_index("zl")
    starts = (jnp.cumsum(doc_lengths) - doc_lengths - part * (slabs * tok_dev)).reshape(1, -1)
    starts = starts.astype(jnp.float32)

    keys = split_keys(section_token_rows, row_target, tp_count)
    keys = exchange(keys, "tp").reshape(tok_dev, KEY_CHUNK)
    keys, forward, backward = sort_rows(keys, parts, per_pair)
    load, value, places = arrange(exchange(keys, PART), per_pair)
    load, value, rows = lax.optimization_barrier((load, value, section_token_rows))
    queries = exchange(split_queries(rows, tp_count), "tp").reshape(tok_dev, QUERY_WIDTH)

    def passed(block, sign):
        route = []
        for at in range(slabs):
            for low in range(2):
                to = (at + sign * (1 - 2 * low)) % slabs
                route.append((at * 2 + low, to * 2 + low))
        return lax.ppermute(block, RING, route)

    loads, values = [load], [value]
    load_a, load_b, value_a, value_b = load, load, value, value
    for step in range(1, slabs // 2):
        load_a = passed(load_a, 1)
        load_b = passed(load_b, -1)
        value_a, value_b = passed(value_a, 1), passed(value_b, -1)
        if step in MEETINGS:
            load_a, load_b, value_a, value_b, queries = lax.optimization_barrier(
                (load_a, load_b, value_a, value_b, queries)
            )
        if step == MEETINGS[0]:
            queries = permute_rows(forward, queries, "sort_queries")
            queries = exchange(queries.reshape(parts, tok_dev // parts, QUERY_WIDTH), PART)
        loads += [load_a, load_b]
        values += [value_a, value_b]
    loads.append(passed(load_a, 1))
    values.append(passed(value_b, -1))
    queries = queries.reshape(parts, slabs, per_pair, QUERY_WIDTH).transpose(1, 0, 2, 3)
    queries = queries.reshape(tok_dev, QUERY_WIDTH)

    done = attend(starts, places, queries, loads, values, parts, per_pair)
    back = exchange(done, PART).reshape(tok_dev, QUERY_WIDTH)
    back = permute_rows(backward, back, "unsort").reshape(tp_count, local_rows, QUERY_WIDTH)
    back = exchange(back, "tp")
    return back.transpose(1, 0, 2).reshape(local_rows, tp_count * QUERY_WIDTH)


def solution(mesh):
    shape = (4, 8, 2, mesh.shape["tp"])
    ring_mesh = Mesh(mesh.devices.reshape(shape), AXES)
    placed = (P(AXES, None), P(AXES), P())
    return jax.shard_map(
        per_device, mesh=ring_mesh, in_specs=placed, out_specs=P(AXES, None), check_vma=False
    )
```

```python
import functools
import math

import jax
import jax.numpy as jnp
from jax import lax
from jax.experimental import pallas as pl
from jax.experimental.pallas import tpu as pltpu
from jax.sharding import Mesh
from jax.sharding import PartitionSpec as P

HEAD_SIZE = 128
QUERY_PER_KEY = 5
LANES = 128
BLOCK = 512
QUERY_WIDTH = QUERY_PER_KEY * HEAD_SIZE
KV_WIDTH = 2 * HEAD_SIZE
KEY_CHUNK = KV_WIDTH + LANES
MASKED = -1e30
VMEM_LIMIT = 24 * 1024 * 1024
AXES = ("x", "zh", "zl", "tp")
PART = ("x", "zl")
RING = ("zh", "zl")


def whole(n):
    return [pl.BlockSpec(memory_space=pltpu.VMEM)] * n


def params():
    return pltpu.CompilerParams(vmem_limit_bytes=VMEM_LIMIT)


def cost(flops, moved):
    return pl.CostEstimate(flops=flops, bytes_accessed=moved, transcendentals=0)


def iota(shape, axis):
    return lax.broadcasted_iota(jnp.int32, shape, axis)


def eye(n):
    return iota((n, n), 0) == iota((n, n), 1)


def column_to_row(column):
    n = column.shape[0]
    return jnp.sum(jnp.where(eye(n), column, 0.0), axis=0, keepdims=True)


def split_keys_kernel(target_ref, key_ref, value_ref, out_ref):
    n = key_ref.shape[0]
    target = jnp.sum(jnp.where(eye(n), target_ref[...], 0), axis=1, keepdims=True)
    lane = iota((n, LANES), 1)
    coded = jnp.where(lane == 0, target >> 8, jnp.where(lane == 1, target & 255, 0))
    out_ref[0, :, :HEAD_SIZE] = key_ref[...]
    out_ref[0, :, HEAD_SIZE:KV_WIDTH] = value_ref[...]
    out_ref[0, :, KV_WIDTH:] = coded.astype(jnp.float32).astype(jnp.bfloat16)


def split_keys(rows, target, groups):
    n = rows.shape[0]
    heads = QUERY_PER_KEY + 2
    return pl.pallas_call(
        split_keys_kernel,
        grid=(groups,),
        in_specs=[
            pl.BlockSpec((1, n), lambda g: (0, 0)),
            pl.BlockSpec((n, HEAD_SIZE), lambda g: (0, heads * g + QUERY_PER_KEY)),
            pl.BlockSpec((n, HEAD_SIZE), lambda g: (0, heads * g + QUERY_PER_KEY + 1)),
        ],
        out_specs=pl.BlockSpec((1, n, KEY_CHUNK), lambda g: (g, 0, 0)),
        out_shape=jax.ShapeDtypeStruct((groups, n, KEY_CHUNK), rows.dtype),
        compiler_params=params(),
        cost_estimate=cost(0, 4 * groups * n * KEY_CHUNK),
        name="split_keys",
    )(target.reshape(1, n), rows, rows)


def split_queries_kernel(rows_ref, out_ref):
    out_ref[0] = rows_ref[:, :QUERY_WIDTH]


def split_queries(rows, groups):
    n, width = rows.shape
    return pl.pallas_call(
        split_queries_kernel,
        grid=(groups,),
        in_specs=[pl.BlockSpec((n, width // groups), lambda g: (0, g))],
        out_specs=pl.BlockSpec((1, n, QUERY_WIDTH), lambda g: (g, 0, 0)),
        out_shape=jax.ShapeDtypeStruct((groups, n, QUERY_WIDTH), rows.dtype),
        compiler_params=params(),
        cost_estimate=cost(0, 4 * rows.size),
        name="split_queries",
    )(rows)


def sort_kernel(per_pair, chunk_ref, keys_ref, forward_ref, backward_ref):
    n = chunk_ref.shape[0]
    parts, padded, _ = keys_ref.shape
    coded = chunk_ref[:, KV_WIDTH:].astype(jnp.float32)
    column = coded[:, 0:1] * 256.0 + coded[:, 1:2]
    row = column_to_row(column)
    rank_row = jnp.sum(jnp.where(column < row, 1.0, 0.0), axis=0, keepdims=True)
    rank_column = jnp.sum(jnp.where(row < column, 1.0, 0.0), axis=1, keepdims=True)
    down = iota((n, n), 0).astype(jnp.float32)
    across = iota((n, n), 1).astype(jnp.float32)
    forward_ref[...] = jnp.where(rank_row == down, 1.0, 0.0).astype(jnp.bfloat16)
    backward_ref[...] = jnp.where(rank_column == across, 1.0, 0.0).astype(jnp.bfloat16)
    local = jnp.where(coded[:, 0:1] - 2.0 * jnp.floor(coded[:, 0:1] * 0.5) > 0.5, 0.0, -256.0)
    local = local + coded[:, 1:2]
    tile = jnp.where(iota((n, LANES), 1) == 0, local, 0.0).astype(jnp.bfloat16)
    wanted = jnp.concatenate(
        [(iota((padded, n), 0) + (p * (n // parts) - per_pair)) & (n - 1) for p in range(parts)],
        axis=0,
    ).astype(jnp.float32)
    order = jnp.where(rank_row == wanted, 1.0, 0.0).astype(jnp.bfloat16)
    keys = jnp.dot(order, chunk_ref[:, :KV_WIDTH], preferred_element_type=jnp.float32)
    places = jnp.dot(order, tile, preferred_element_type=jnp.float32)
    for p in range(parts):
        rows = slice(p * padded, (p + 1) * padded)
        keys_ref[p, :, :KV_WIDTH] = keys[rows].astype(keys_ref.dtype)
        keys_ref[p, :, KV_WIDTH:] = places[rows].astype(keys_ref.dtype)


def sort_rows(chunk, parts, per_pair):
    n = chunk.shape[0]
    padded = n // parts + per_pair
    return pl.pallas_call(
        functools.partial(sort_kernel, per_pair),
        in_specs=whole(1),
        out_specs=whole(3),
        out_shape=[
            jax.ShapeDtypeStruct((parts, padded, KEY_CHUNK), chunk.dtype),
            jax.ShapeDtypeStruct((n, n), jnp.bfloat16),
            jax.ShapeDtypeStruct((n, n), jnp.bfloat16),
        ],
        compiler_params=params(),
        cost_estimate=cost(2 * n * chunk.size, 4 * chunk.size),
        name="sort_rows",
    )(chunk)


def permute_kernel(order_ref, chunk_ref, out_ref):
    out_ref[...] = jnp.dot(
        order_ref[...], chunk_ref[...], preferred_element_type=jnp.float32
    ).astype(out_ref.dtype)


def permute_rows(order, chunk):
    return pl.pallas_call(
        permute_kernel,
        in_specs=whole(2),
        out_specs=pl.BlockSpec(memory_space=pltpu.VMEM),
        out_shape=jax.ShapeDtypeStruct(chunk.shape, chunk.dtype),
        compiler_params=params(),
        cost_estimate=cost(2 * chunk.shape[0] * chunk.size, 4 * chunk.size),
    )(order, chunk)


def arrange_kernel(per_pair, got_ref, key_ref, value_ref, place_ref):
    sources, padded, _ = got_ref.shape
    blocks = padded // per_pair
    span = sources * per_pair
    pieces = [got_ref[s].astype(jnp.float32) for s in range(sources)]
    places = []
    for b in range(blocks):
        rows = slice(b * per_pair, (b + 1) * per_pair)
        block = jnp.concatenate([piece[rows] for piece in pieces], axis=0)
        at = slice(b * span, (b + 1) * span)
        key_ref[at, :] = block[:, :HEAD_SIZE].astype(key_ref.dtype)
        value_ref[at, :] = block[:, HEAD_SIZE:KV_WIDTH].astype(value_ref.dtype)
        places.append(block[:, KV_WIDTH:])
        place_ref[at, :] = places[b]
    rows = jnp.zeros((16, LANES), jnp.float32)
    for b in range(1, blocks):
        pair = jnp.concatenate([places[b - 1], places[b]], axis=0)[:, 0:1]
        rows = jnp.where(iota((16, LANES), 0) == b - 1, column_to_row(pair), rows)
    key_ref[blocks * span :, :] = rows.astype(key_ref.dtype)


def arrange(got, per_pair):
    sources, padded, _ = got.shape
    rows = sources * padded
    return pl.pallas_call(
        functools.partial(arrange_kernel, per_pair),
        in_specs=whole(1),
        out_specs=whole(3),
        out_shape=[
            jax.ShapeDtypeStruct((rows + 16, HEAD_SIZE), got.dtype),
            jax.ShapeDtypeStruct((rows, HEAD_SIZE), got.dtype),
            jax.ShapeDtypeStruct((rows, LANES), jnp.float32),
        ],
        compiler_params=params(),
        cost_estimate=cost(0, 4 * got.size),
        name="arrange",
    )(got)


def attend_kernel(per_pair, loads, starts_ref, place_ref, query_ref, *refs):
    load_refs, value_refs = refs[:loads], refs[loads : 2 * loads]
    out_ref, key_ref, value_ref, done_ref = refs[2 * loads :]
    sources = out_ref.shape[0]
    span = sources * per_pair
    blocks = out_ref.shape[1] // per_pair
    pair = 2 * span
    scale = math.log2(math.e) / math.sqrt(HEAD_SIZE)
    half = float(BLOCK // 2)
    lane = iota((1, pair), 1)
    shift = jnp.where(lane < span, half - BLOCK, half)
    starts = starts_ref[...]
    for b in range(blocks):
        rows = slice(b * span, b * span + pair)
        for at in range(loads):
            key_ref[at * pair : (at + 1) * pair, :] = load_refs[at][rows, :]
            value_ref[at * pair : (at + 1) * pair, :] = value_refs[at][rows, :]
        key_place = jnp.concatenate(
            [
                load_ref[(blocks + 1) * span :, :].astype(jnp.float32)[b : b + 1] + shift
                for load_ref in load_refs
            ],
            axis=1,
        )
        place = place_ref[(b + 1) * span : (b + 2) * span, 0:1] + half
        base = float(b * BLOCK)
        start = jnp.max(
            jnp.where(starts <= place + base, starts, -1e9), axis=1, keepdims=True
        )
        allowed = (key_place >= start - base) & (key_place <= place)
        bias = jnp.where(allowed, 0.0, MASKED)
        query = query_ref[b * span : (b + 1) * span, :]
        query = jnp.concatenate(
            [query[:, h * HEAD_SIZE : (h + 1) * HEAD_SIZE] for h in range(QUERY_PER_KEY)], axis=0
        )
        scores = lax.dot_general(
            query, key_ref[...], (((1,), (1,)), ((), ())), preferred_element_type=jnp.float32
        )
        scores = scores.reshape(QUERY_PER_KEY, span, loads * pair) * scale + bias[None]
        weights = jnp.exp2(scores - jnp.max(scores, axis=2, keepdims=True))
        total = jnp.sum(weights, axis=2, keepdims=True).reshape(QUERY_PER_KEY * span, 1)
        weights = weights.astype(jnp.bfloat16).reshape(QUERY_PER_KEY * span, loads * pair)
        done = jnp.dot(weights, value_ref[...], preferred_element_type=jnp.float32) / total
        for h in range(QUERY_PER_KEY):
            for s in range(sources):
                first = h * span + s * per_pair
                done_ref[
                    s, b * per_pair : (b + 1) * per_pair, h * HEAD_SIZE : (h + 1) * HEAD_SIZE
                ] = done[first : first + per_pair]
    out_ref[...] = done_ref[...].astype(out_ref.dtype)


def attend(starts, places, queries, loads, values, sources, per_pair):
    n = queries.shape[0]
    keys = len(loads) * 2 * sources * per_pair
    shape = (sources, n // sources, QUERY_WIDTH)
    return pl.pallas_call(
        functools.partial(attend_kernel, per_pair, len(loads)),
        in_specs=whole(3 + 2 * len(loads)),
        out_specs=pl.BlockSpec(memory_space=pltpu.VMEM),
        out_shape=jax.ShapeDtypeStruct(shape, queries.dtype),
        scratch_shapes=[
            pltpu.VMEM((keys, HEAD_SIZE), queries.dtype),
            pltpu.VMEM((keys, HEAD_SIZE), queries.dtype),
            pltpu.VMEM(shape, jnp.float32),
        ],
        compiler_params=params(),
        cost_estimate=cost(4 * n * keys * QUERY_WIDTH, 4 * n * QUERY_WIDTH),
        name="attend",
    )(starts, places, queries, *loads, *values)


def exchange(blocks, axis):
    return lax.all_to_all(blocks, axis, split_axis=0, concat_axis=0, tiled=True)


def per_device(section_token_rows, row_target, doc_lengths):
    tp_count = lax.axis_size("tp")
    slabs = lax.axis_size("zh")
    parts = lax.axis_size("x") * lax.axis_size("zl")
    local_rows = section_token_rows.shape[0]
    tok_dev = local_rows * tp_count
    per_pair = tok_dev // (parts * slabs)
    part = lax.axis_index("x") * lax.axis_size("zl") + lax.axis_index("zl")
    starts = (jnp.cumsum(doc_lengths) - doc_lengths - part * (slabs * tok_dev)).reshape(1, -1)
    starts = starts.astype(jnp.float32)

    keys = split_keys(section_token_rows, row_target, tp_count)
    keys = exchange(keys, "tp").reshape(tok_dev, KEY_CHUNK)
    keys, forward, backward = sort_rows(keys, parts, per_pair)
    load, value, places = arrange(exchange(keys, PART), per_pair)

    load, value, rows = lax.optimization_barrier((load, value, section_token_rows))
    queries = split_queries(rows, tp_count)
    queries = exchange(queries, "tp").reshape(tok_dev, QUERY_WIDTH)
    queries = permute_rows(forward, queries)
    queries = exchange(queries.reshape(parts, tok_dev // parts, QUERY_WIDTH), PART)
    queries = queries.reshape(parts, slabs, per_pair, QUERY_WIDTH).transpose(1, 0, 2, 3)
    queries = queries.reshape(tok_dev, QUERY_WIDTH)

    def passed(block, sign):
        route = []
        for at in range(slabs):
            for low in range(2):
                to = (at + sign * (1 - 2 * low)) % slabs
                route.append((at * 2 + low, to * 2 + low))
        return lax.ppermute(block, RING, route)

    loads, values = [load], [value]
    load_a, load_b, value_a, value_b = load, load, value, value
    for _ in range(1, slabs // 2):
        load_a, load_b = passed(load_a, 1), passed(load_b, -1)
        value_a, value_b = passed(value_a, 1), passed(value_b, -1)
        loads += [load_a, load_b]
        values += [value_a, value_b]
    loads.append(passed(load_a, 1))
    values.append(passed(value_b, -1))

    done = attend(starts, places, queries, loads, values, parts, per_pair)
    back = exchange(done, PART).reshape(tok_dev, QUERY_WIDTH)
    back = permute_rows(backward, back).reshape(tp_count, local_rows, QUERY_WIDTH)
    back = exchange(back, "tp")
    return back.transpose(1, 0, 2).reshape(local_rows, tp_count * QUERY_WIDTH)


def solution(mesh):
    shape = (4, 8, 2, mesh.shape["tp"])
    ring_mesh = Mesh(mesh.devices.reshape(shape), AXES)
    placed = (P(AXES, None), P(AXES), P())
    return jax.shard_map(
        per_device, mesh=ring_mesh, in_specs=placed, out_specs=P(AXES, None), check_vma=False
    )
```

```python
import functools
import math

import jax
import jax.numpy as jnp
from jax import lax
from jax.experimental import pallas as pl
from jax.experimental.pallas import tpu as pltpu
from jax.sharding import Mesh
from jax.sharding import PartitionSpec as P

HEAD_SIZE = 128
QUERY_PER_KEY = 5
LANES = 128
BLOCK = 512
QUERY_WIDTH = QUERY_PER_KEY * HEAD_SIZE
KV_WIDTH = 2 * HEAD_SIZE
KEY_CHUNK = KV_WIDTH + LANES
MASKED = -1e30
VMEM_LIMIT = 24 * 1024 * 1024
AXES = ("x", "zh", "zl", "tp")
PART = ("x", "zl")
RING = ("zh", "zl")


def whole(n):
    return [pl.BlockSpec(memory_space=pltpu.VMEM)] * n


def params():
    return pltpu.CompilerParams(vmem_limit_bytes=VMEM_LIMIT)


def cost(flops, moved):
    return pl.CostEstimate(flops=flops, bytes_accessed=moved, transcendentals=0)


def iota(shape, axis):
    return lax.broadcasted_iota(jnp.int32, shape, axis)


def eye(n):
    return iota((n, n), 0) == iota((n, n), 1)


def column_to_row(column):
    n = column.shape[0]
    return jnp.sum(jnp.where(eye(n), column, 0.0), axis=0, keepdims=True)


def split_keys_kernel(target_ref, key_ref, value_ref, out_ref):
    n = key_ref.shape[0]
    target = jnp.sum(jnp.where(eye(n), target_ref[...], 0), axis=1, keepdims=True)
    lane = iota((n, LANES), 1)
    coded = jnp.where(lane == 0, target >> 8, jnp.where(lane == 1, target & 255, 0))
    out_ref[0, :, :HEAD_SIZE] = key_ref[...]
    out_ref[0, :, HEAD_SIZE:KV_WIDTH] = value_ref[...]
    out_ref[0, :, KV_WIDTH:] = coded.astype(jnp.float32).astype(jnp.bfloat16)


def split_keys(rows, target, groups):
    n = rows.shape[0]
    heads = QUERY_PER_KEY + 2
    return pl.pallas_call(
        split_keys_kernel,
        grid=(groups,),
        in_specs=[
            pl.BlockSpec((1, n), lambda g: (0, 0)),
            pl.BlockSpec((n, HEAD_SIZE), lambda g: (0, heads * g + QUERY_PER_KEY)),
            pl.BlockSpec((n, HEAD_SIZE), lambda g: (0, heads * g + QUERY_PER_KEY + 1)),
        ],
        out_specs=pl.BlockSpec((1, n, KEY_CHUNK), lambda g: (g, 0, 0)),
        out_shape=jax.ShapeDtypeStruct((groups, n, KEY_CHUNK), rows.dtype),
        compiler_params=params(),
        cost_estimate=cost(0, 4 * groups * n * KEY_CHUNK),
        name="split_keys",
    )(target.reshape(1, n), rows, rows)


def split_queries_kernel(rows_ref, out_ref):
    out_ref[0] = rows_ref[:, :QUERY_WIDTH]


def split_queries(rows, groups):
    n, width = rows.shape
    return pl.pallas_call(
        split_queries_kernel,
        grid=(groups,),
        in_specs=[pl.BlockSpec((n, width // groups), lambda g: (0, g))],
        out_specs=pl.BlockSpec((1, n, QUERY_WIDTH), lambda g: (g, 0, 0)),
        out_shape=jax.ShapeDtypeStruct((groups, n, QUERY_WIDTH), rows.dtype),
        compiler_params=params(),
        cost_estimate=cost(0, 4 * rows.size),
        name="split_queries",
    )(rows)


def sort_kernel(per_pair, chunk_ref, keys_ref, forward_ref, backward_ref):
    n = chunk_ref.shape[0]
    parts, padded, _ = keys_ref.shape
    coded = chunk_ref[:, KV_WIDTH:].astype(jnp.float32)
    column = coded[:, 0:1] * 256.0 + coded[:, 1:2]
    row = column_to_row(column)
    rank_row = jnp.sum(jnp.where(column < row, 1.0, 0.0), axis=0, keepdims=True)
    rank_column = jnp.sum(jnp.where(row < column, 1.0, 0.0), axis=1, keepdims=True)
    down = iota((n, n), 0).astype(jnp.float32)
    across = iota((n, n), 1).astype(jnp.float32)
    forward_ref[...] = jnp.where(rank_row == down, 1.0, 0.0).astype(jnp.bfloat16)
    backward_ref[...] = jnp.where(rank_column == across, 1.0, 0.0).astype(jnp.bfloat16)
    local = jnp.where(coded[:, 0:1] - 2.0 * jnp.floor(coded[:, 0:1] * 0.5) > 0.5, 0.0, -256.0)
    local = local + coded[:, 1:2]
    tile = jnp.where(iota((n, LANES), 1) == 0, local, 0.0).astype(jnp.bfloat16)
    wanted = jnp.concatenate(
        [(iota((padded, n), 0) + (p * (n // parts) - per_pair)) & (n - 1) for p in range(parts)],
        axis=0,
    ).astype(jnp.float32)
    order = jnp.where(rank_row == wanted, 1.0, 0.0).astype(jnp.bfloat16)
    keys = jnp.dot(order, chunk_ref[:, :KV_WIDTH], preferred_element_type=jnp.float32)
    places = jnp.dot(order, tile, preferred_element_type=jnp.float32)
    for p in range(parts):
        rows = slice(p * padded, (p + 1) * padded)
        keys_ref[p, :, :KV_WIDTH] = keys[rows].astype(keys_ref.dtype)
        keys_ref[p, :, KV_WIDTH:] = places[rows].astype(keys_ref.dtype)


def sort_rows(chunk, parts, per_pair):
    n = chunk.shape[0]
    padded = n // parts + per_pair
    return pl.pallas_call(
        functools.partial(sort_kernel, per_pair),
        in_specs=whole(1),
        out_specs=whole(3),
        out_shape=[
            jax.ShapeDtypeStruct((parts, padded, KEY_CHUNK), chunk.dtype),
            jax.ShapeDtypeStruct((n, n), jnp.bfloat16),
            jax.ShapeDtypeStruct((n, n), jnp.bfloat16),
        ],
        compiler_params=params(),
        cost_estimate=cost(2 * n * chunk.size, 4 * chunk.size),
        name="sort_rows",
    )(chunk)


def permute_kernel(order_ref, chunk_ref, out_ref):
    out_ref[...] = jnp.dot(
        order_ref[...], chunk_ref[...], preferred_element_type=jnp.float32
    ).astype(out_ref.dtype)


def permute_rows(order, chunk):
    return pl.pallas_call(
        permute_kernel,
        in_specs=whole(2),
        out_specs=pl.BlockSpec(memory_space=pltpu.VMEM),
        out_shape=jax.ShapeDtypeStruct(chunk.shape, chunk.dtype),
        compiler_params=params(),
        cost_estimate=cost(2 * chunk.shape[0] * chunk.size, 4 * chunk.size),
    )(order, chunk)


def arrange_kernel(per_pair, got_ref, load_ref, place_ref):
    sources, padded, _ = got_ref.shape
    blocks = padded // per_pair
    span = sources * per_pair
    pieces = [got_ref[s].astype(jnp.float32) for s in range(sources)]
    places = []
    for b in range(blocks):
        rows = slice(b * per_pair, (b + 1) * per_pair)
        block = jnp.concatenate([piece[rows] for piece in pieces], axis=0)
        at = slice(b * span, (b + 1) * span)
        load_ref[at, :] = block[:, :KV_WIDTH].astype(load_ref.dtype)
        places.append(block[:, KV_WIDTH:])
        place_ref[at, :] = places[b]
    rows = jnp.zeros((16, LANES), jnp.float32)
    for b in range(1, blocks):
        pair = jnp.concatenate([places[b - 1], places[b]], axis=0)[:, 0:1]
        rows = jnp.where(iota((16, LANES), 0) == b - 1, column_to_row(pair), rows)
    load_ref[blocks * span :, :HEAD_SIZE] = rows.astype(load_ref.dtype)
    load_ref[blocks * span :, HEAD_SIZE:] = jnp.zeros((16, HEAD_SIZE), load_ref.dtype)


def arrange(got, per_pair):
    sources, padded, _ = got.shape
    rows = sources * padded
    return pl.pallas_call(
        functools.partial(arrange_kernel, per_pair),
        in_specs=whole(1),
        out_specs=whole(2),
        out_shape=[
            jax.ShapeDtypeStruct((rows + 16, KV_WIDTH), got.dtype),
            jax.ShapeDtypeStruct((rows, LANES), jnp.float32),
        ],
        compiler_params=params(),
        cost_estimate=cost(0, 4 * got.size),
        name="arrange",
    )(got)


def attend_kernel(per_pair, loads, starts_ref, place_ref, query_ref, *refs):
    load_refs, value_refs = refs[:loads], refs[loads : 2 * loads]
    out_ref, key_ref, value_ref, done_ref = refs[2 * loads :]
    sources = out_ref.shape[0]
    span = sources * per_pair
    blocks = out_ref.shape[1] // per_pair
    pair = 2 * span
    scale = math.log2(math.e) / math.sqrt(HEAD_SIZE)
    half = float(BLOCK // 2)
    lane = iota((1, pair), 1)
    shift = jnp.where(lane < span, half - BLOCK, half)
    starts = starts_ref[...]
    for b in range(blocks):
        rows = slice(b * span, b * span + pair)
        for at in range(loads):
            key_ref[at * pair : (at + 1) * pair, :] = load_refs[at][rows, :HEAD_SIZE]
            value_ref[at * pair : (at + 1) * pair, :] = value_refs[at][rows, -HEAD_SIZE:]
        key_place = jnp.concatenate(
            [
                load_ref[(blocks + 1) * span :, :LANES].astype(jnp.float32)[b : b + 1] + shift
                for load_ref in load_refs
            ],
            axis=1,
        )
        place = place_ref[(b + 1) * span : (b + 2) * span, 0:1] + half
        base = float(b * BLOCK)
        start = jnp.max(
            jnp.where(starts <= place + base, starts, -1e9), axis=1, keepdims=True
        )
        allowed = (key_place >= start - base) & (key_place <= place)
        bias = jnp.where(allowed, 0.0, MASKED)
        query = query_ref[b * span : (b + 1) * span, :]
        query = jnp.concatenate(
            [query[:, h * HEAD_SIZE : (h + 1) * HEAD_SIZE] for h in range(QUERY_PER_KEY)], axis=0
        )
        scores = lax.dot_general(
            query, key_ref[...], (((1,), (1,)), ((), ())), preferred_element_type=jnp.float32
        )
        scores = scores.reshape(QUERY_PER_KEY, span, loads * pair) * scale + bias[None]
        weights = jnp.exp2(scores - jnp.max(scores, axis=2, keepdims=True))
        total = jnp.sum(weights, axis=2, keepdims=True).reshape(QUERY_PER_KEY * span, 1)
        weights = weights.astype(jnp.bfloat16).reshape(QUERY_PER_KEY * span, loads * pair)
        done = jnp.dot(weights, value_ref[...], preferred_element_type=jnp.float32) / total
        for h in range(QUERY_PER_KEY):
            for s in range(sources):
                first = h * span + s * per_pair
                done_ref[
                    s, b * per_pair : (b + 1) * per_pair, h * HEAD_SIZE : (h + 1) * HEAD_SIZE
                ] = done[first : first + per_pair]
    out_ref[...] = done_ref[...].astype(out_ref.dtype)


def attend(starts, places, queries, loads, values, sources, per_pair):
    n = queries.shape[0]
    keys = len(loads) * 2 * sources * per_pair
    shape = (sources, n // sources, QUERY_WIDTH)
    return pl.pallas_call(
        functools.partial(attend_kernel, per_pair, len(loads)),
        in_specs=whole(3 + 2 * len(loads)),
        out_specs=pl.BlockSpec(memory_space=pltpu.VMEM),
        out_shape=jax.ShapeDtypeStruct(shape, queries.dtype),
        scratch_shapes=[
            pltpu.VMEM((keys, HEAD_SIZE), queries.dtype),
            pltpu.VMEM((keys, HEAD_SIZE), queries.dtype),
            pltpu.VMEM(shape, jnp.float32),
        ],
        compiler_params=params(),
        cost_estimate=cost(4 * n * keys * QUERY_WIDTH, 4 * n * QUERY_WIDTH),
        name="attend",
    )(starts, places, queries, *loads, *values)


def exchange(blocks, axis):
    return lax.all_to_all(blocks, axis, split_axis=0, concat_axis=0, tiled=True)


def per_device(section_token_rows, row_target, doc_lengths):
    tp_count = lax.axis_size("tp")
    slabs = lax.axis_size("zh")
    parts = lax.axis_size("x") * lax.axis_size("zl")
    local_rows = section_token_rows.shape[0]
    tok_dev = local_rows * tp_count
    per_pair = tok_dev // (parts * slabs)
    part = lax.axis_index("x") * lax.axis_size("zl") + lax.axis_index("zl")
    starts = (jnp.cumsum(doc_lengths) - doc_lengths - part * (slabs * tok_dev)).reshape(1, -1)
    starts = starts.astype(jnp.float32)

    keys = split_keys(section_token_rows, row_target, tp_count)
    keys = exchange(keys, "tp").reshape(tok_dev, KEY_CHUNK)
    keys, forward, backward = sort_rows(keys, parts, per_pair)
    load, places = arrange(exchange(keys, PART), per_pair)

    load, rows = lax.optimization_barrier((load, section_token_rows))
    queries = split_queries(rows, tp_count)
    queries = exchange(queries, "tp").reshape(tok_dev, QUERY_WIDTH)
    queries = permute_rows(forward, queries)
    queries = exchange(queries.reshape(parts, tok_dev // parts, QUERY_WIDTH), PART)
    queries = queries.reshape(parts, slabs, per_pair, QUERY_WIDTH).transpose(1, 0, 2, 3)
    queries = queries.reshape(tok_dev, QUERY_WIDTH)

    def passed(block, sign):
        route = []
        for at in range(slabs):
            for low in range(2):
                to = (at + sign * (1 - 2 * low)) % slabs
                route.append((at * 2 + low, to * 2 + low))
        return lax.ppermute(block, RING, route)

    loads = [load]
    load_a, load_b = load, load
    for _ in range(1, slabs // 2):
        load_a, load_b = passed(load_a, 1), passed(load_b, -1)
        loads += [load_a, load_b]
    values = loads + [passed(load_b[:, HEAD_SIZE:], -1)]
    loads = loads + [passed(load_a[:, :HEAD_SIZE], 1)]

    done = attend(starts, places, queries, loads, values, parts, per_pair)
    back = exchange(done, PART).reshape(tok_dev, QUERY_WIDTH)
    back = permute_rows(backward, back).reshape(tp_count, local_rows, QUERY_WIDTH)
    back = exchange(back, "tp")
    return back.transpose(1, 0, 2).reshape(local_rows, tp_count * QUERY_WIDTH)


def solution(mesh):
    shape = (4, 8, 2, mesh.shape["tp"])
    ring_mesh = Mesh(mesh.devices.reshape(shape), AXES)
    placed = (P(AXES, None), P(AXES), P())
    return jax.shard_map(
        per_device, mesh=ring_mesh, in_specs=placed, out_specs=P(AXES, None), check_vma=False
    )
```

```python
import functools
import math

import jax
import jax.numpy as jnp
from jax import lax
from jax.experimental import pallas as pl
from jax.experimental.pallas import tpu as pltpu
from jax.sharding import Mesh
from jax.sharding import PartitionSpec as P

HEAD_SIZE = 128
QUERY_PER_KEY = 5
LANES = 128
BLOCK = 512
QUERY_WIDTH = QUERY_PER_KEY * HEAD_SIZE
KV_WIDTH = 2 * HEAD_SIZE
KEY_CHUNK = KV_WIDTH + LANES
MASKED = -1e30
VMEM_LIMIT = 24 * 1024 * 1024
AXES = ("x", "zh", "zl", "tp")
PART = ("x", "zl")
RING = ("zh", "zl")


def whole(n):
    return [pl.BlockSpec(memory_space=pltpu.VMEM)] * n


def params():
    return pltpu.CompilerParams(vmem_limit_bytes=VMEM_LIMIT)


def cost(flops, moved):
    return pl.CostEstimate(flops=flops, bytes_accessed=moved, transcendentals=0)


def iota(shape, axis):
    return lax.broadcasted_iota(jnp.int32, shape, axis)


def eye(n):
    return iota((n, n), 0) == iota((n, n), 1)


def column_to_row(column):
    n = column.shape[0]
    return jnp.sum(jnp.where(eye(n), column, 0.0), axis=0, keepdims=True)


def split_keys_kernel(target_ref, key_ref, value_ref, out_ref):
    n = key_ref.shape[0]
    target = jnp.sum(jnp.where(eye(n), target_ref[...], 0), axis=1, keepdims=True)
    lane = iota((n, LANES), 1)
    coded = jnp.where(lane == 0, target >> 8, jnp.where(lane == 1, target & 255, 0))
    out_ref[0, :, :HEAD_SIZE] = key_ref[...]
    out_ref[0, :, HEAD_SIZE:KV_WIDTH] = value_ref[...]
    out_ref[0, :, KV_WIDTH:] = coded.astype(jnp.float32).astype(jnp.bfloat16)


def split_keys(rows, target, groups):
    n = rows.shape[0]
    heads = QUERY_PER_KEY + 2
    return pl.pallas_call(
        split_keys_kernel,
        grid=(groups,),
        in_specs=[
            pl.BlockSpec((1, n), lambda g: (0, 0)),
            pl.BlockSpec((n, HEAD_SIZE), lambda g: (0, heads * g + QUERY_PER_KEY)),
            pl.BlockSpec((n, HEAD_SIZE), lambda g: (0, heads * g + QUERY_PER_KEY + 1)),
        ],
        out_specs=pl.BlockSpec((1, n, KEY_CHUNK), lambda g: (g, 0, 0)),
        out_shape=jax.ShapeDtypeStruct((groups, n, KEY_CHUNK), rows.dtype),
        compiler_params=params(),
        cost_estimate=cost(0, 4 * groups * n * KEY_CHUNK),
        name="split_keys",
    )(target.reshape(1, n), *[pltpu.with_memory_space_constraint(rows, pltpu.HBM)] * 2)


def split_queries_kernel(rows_ref, out_ref):
    out_ref[0] = rows_ref[:, :QUERY_WIDTH]


def split_queries(rows, groups):
    n, width = rows.shape
    return pl.pallas_call(
        split_queries_kernel,
        grid=(groups,),
        in_specs=[pl.BlockSpec((n, width // groups), lambda g: (0, g))],
        out_specs=pl.BlockSpec((1, n, QUERY_WIDTH), lambda g: (g, 0, 0)),
        out_shape=jax.ShapeDtypeStruct((groups, n, QUERY_WIDTH), rows.dtype),
        compiler_params=params(),
        cost_estimate=cost(0, 4 * rows.size),
        name="split_queries",
    )(rows)


def sort_kernel(per_pair, chunk_ref, keys_ref, forward_ref, backward_ref):
    n = chunk_ref.shape[0]
    parts, padded, _ = keys_ref.shape
    coded = chunk_ref[:, KV_WIDTH:].astype(jnp.float32)
    column = coded[:, 0:1] * 256.0 + coded[:, 1:2]
    row = column_to_row(column)
    rank_row = jnp.sum(jnp.where(column < row, 1.0, 0.0), axis=0, keepdims=True)
    rank_column = jnp.sum(jnp.where(row < column, 1.0, 0.0), axis=1, keepdims=True)
    down = iota((n, n), 0).astype(jnp.float32)
    across = iota((n, n), 1).astype(jnp.float32)
    forward_ref[...] = jnp.where(rank_row == down, 1.0, 0.0).astype(jnp.bfloat16)
    backward_ref[...] = jnp.where(rank_column == across, 1.0, 0.0).astype(jnp.bfloat16)
    local = jnp.where(coded[:, 0:1] - 2.0 * jnp.floor(coded[:, 0:1] * 0.5) > 0.5, 0.0, -256.0)
    local = local + coded[:, 1:2]
    tile = jnp.where(iota((n, LANES), 1) == 0, local, 0.0).astype(jnp.bfloat16)
    wanted = jnp.concatenate(
        [(iota((padded, n), 0) + (p * (n // parts) - per_pair)) & (n - 1) for p in range(parts)],
        axis=0,
    ).astype(jnp.float32)
    order = jnp.where(rank_row == wanted, 1.0, 0.0).astype(jnp.bfloat16)
    keys = jnp.dot(order, chunk_ref[:, :KV_WIDTH], preferred_element_type=jnp.float32)
    places = jnp.dot(order, tile, preferred_element_type=jnp.float32)
    for p in range(parts):
        rows = slice(p * padded, (p + 1) * padded)
        keys_ref[p, :, :KV_WIDTH] = keys[rows].astype(keys_ref.dtype)
        keys_ref[p, :, KV_WIDTH:] = places[rows].astype(keys_ref.dtype)


def sort_rows(chunk, parts, per_pair):
    n = chunk.shape[0]
    padded = n // parts + per_pair
    return pl.pallas_call(
        functools.partial(sort_kernel, per_pair),
        in_specs=whole(1),
        out_specs=whole(3),
        out_shape=[
            jax.ShapeDtypeStruct((parts, padded, KEY_CHUNK), chunk.dtype),
            jax.ShapeDtypeStruct((n, n), jnp.bfloat16),
            jax.ShapeDtypeStruct((n, n), jnp.bfloat16),
        ],
        compiler_params=params(),
        cost_estimate=cost(2 * n * chunk.size, 4 * chunk.size),
        name="sort_rows",
    )(chunk)


def permute_kernel(order_ref, chunk_ref, out_ref):
    out_ref[...] = jnp.dot(
        order_ref[...], chunk_ref[...], preferred_element_type=jnp.float32
    ).astype(out_ref.dtype)


def permute_rows(order, chunk):
    return pl.pallas_call(
        permute_kernel,
        in_specs=whole(2),
        out_specs=pl.BlockSpec(memory_space=pltpu.VMEM),
        out_shape=jax.ShapeDtypeStruct(chunk.shape, chunk.dtype),
        compiler_params=params(),
        cost_estimate=cost(2 * chunk.shape[0] * chunk.size, 4 * chunk.size),
    )(order, chunk)


def arrange_kernel(per_pair, got_ref, load_ref, place_ref):
    sources, padded, _ = got_ref.shape
    blocks = padded // per_pair
    span = sources * per_pair
    pieces = [got_ref[s].astype(jnp.float32) for s in range(sources)]
    places = []
    for b in range(blocks):
        rows = slice(b * per_pair, (b + 1) * per_pair)
        block = jnp.concatenate([piece[rows] for piece in pieces], axis=0)
        at = slice(b * span, (b + 1) * span)
        load_ref[at, :] = block[:, :KV_WIDTH].astype(load_ref.dtype)
        places.append(block[:, KV_WIDTH:])
        place_ref[at, :] = places[b]
    rows = jnp.zeros((8, LANES), jnp.float32)
    for b in range(1, blocks):
        pair = jnp.concatenate([places[b - 1], places[b]], axis=0)[:, 0:1]
        rows = jnp.where(iota((8, LANES), 0) == b - 1, column_to_row(pair), rows)
    load_ref[blocks * span :, :HEAD_SIZE] = rows.astype(load_ref.dtype)
    load_ref[blocks * span :, HEAD_SIZE:] = jnp.zeros((8, HEAD_SIZE), load_ref.dtype)


def arrange(got, per_pair):
    sources, padded, _ = got.shape
    rows = sources * padded
    return pl.pallas_call(
        functools.partial(arrange_kernel, per_pair),
        in_specs=whole(1),
        out_specs=whole(2),
        out_shape=[
            jax.ShapeDtypeStruct((rows + 8, KV_WIDTH), got.dtype),
            jax.ShapeDtypeStruct((rows, LANES), jnp.float32),
        ],
        compiler_params=params(),
        cost_estimate=cost(0, 4 * got.size),
        name="arrange",
    )(got)


def attend_kernel(per_pair, loads, starts_ref, place_ref, query_ref, *refs):
    load_refs, value_refs = refs[:loads], refs[loads : 2 * loads]
    out_ref, key_ref, value_ref, done_ref = refs[2 * loads :]
    sources = out_ref.shape[0]
    span = sources * per_pair
    blocks = out_ref.shape[1] // per_pair
    pair = 2 * span
    scale = math.log2(math.e) / math.sqrt(HEAD_SIZE)
    half = float(BLOCK // 2)
    lane = iota((1, pair), 1)
    shift = jnp.where(lane < span, half - BLOCK, half)
    starts = starts_ref[...]
    for b in range(blocks):
        rows = slice(b * span, b * span + pair)
        for at in range(loads):
            key_ref[at * pair : (at + 1) * pair, :] = load_refs[at][rows, :HEAD_SIZE]
            value_ref[at * pair : (at + 1) * pair, :] = value_refs[at][rows, -HEAD_SIZE:]
        key_place = jnp.concatenate(
            [
                load_ref[(blocks + 1) * span :, :LANES].astype(jnp.float32)[b : b + 1] + shift
                for load_ref in load_refs
            ],
            axis=1,
        )
        place = place_ref[(b + 1) * span : (b + 2) * span, 0:1] + half
        base = float(b * BLOCK)
        start = jnp.max(
            jnp.where(starts <= place + base, starts, -1e9), axis=1, keepdims=True
        )
        allowed = (key_place >= start - base) & (key_place <= place)
        bias = jnp.where(allowed, 0.0, MASKED)
        query = query_ref[b * span : (b + 1) * span, :]
        query = jnp.concatenate(
            [query[:, h * HEAD_SIZE : (h + 1) * HEAD_SIZE] for h in range(QUERY_PER_KEY)], axis=0
        )
        scores = lax.dot_general(
            query, key_ref[...], (((1,), (1,)), ((), ())), preferred_element_type=jnp.float32
        )
        scores = scores.reshape(QUERY_PER_KEY, span, loads * pair) * scale + bias[None]
        weights = jnp.exp2(scores - jnp.max(scores, axis=2, keepdims=True))
        total = jnp.sum(weights, axis=2, keepdims=True).reshape(QUERY_PER_KEY * span, 1)
        weights = weights.astype(jnp.bfloat16).reshape(QUERY_PER_KEY * span, loads * pair)
        done = jnp.dot(weights, value_ref[...], preferred_element_type=jnp.float32) / total
        for h in range(QUERY_PER_KEY):
            for s in range(sources):
                first = h * span + s * per_pair
                done_ref[
                    s, b * per_pair : (b + 1) * per_pair, h * HEAD_SIZE : (h + 1) * HEAD_SIZE
                ] = done[first : first + per_pair]
    out_ref[...] = done_ref[...].astype(out_ref.dtype)


def attend(starts, places, queries, loads, values, sources, per_pair):
    n = queries.shape[0]
    keys = len(loads) * 2 * sources * per_pair
    shape = (sources, n // sources, QUERY_WIDTH)
    return pl.pallas_call(
        functools.partial(attend_kernel, per_pair, len(loads)),
        in_specs=whole(3 + 2 * len(loads)),
        out_specs=pl.BlockSpec(memory_space=pltpu.VMEM),
        out_shape=jax.ShapeDtypeStruct(shape, queries.dtype),
        scratch_shapes=[
            pltpu.VMEM((keys, HEAD_SIZE), queries.dtype),
            pltpu.VMEM((keys, HEAD_SIZE), queries.dtype),
            pltpu.VMEM(shape, jnp.float32),
        ],
        compiler_params=params(),
        cost_estimate=cost(4 * n * keys * QUERY_WIDTH, 4 * n * QUERY_WIDTH),
        name="attend",
    )(starts, places, queries, *loads, *values)


def exchange(blocks, axis):
    return lax.all_to_all(blocks, axis, split_axis=0, concat_axis=0, tiled=True)


def per_device(section_token_rows, row_target, doc_lengths):
    tp_count = lax.axis_size("tp")
    slabs = lax.axis_size("zh")
    parts = lax.axis_size("x") * lax.axis_size("zl")
    local_rows = section_token_rows.shape[0]
    tok_dev = local_rows * tp_count
    per_pair = tok_dev // (parts * slabs)
    part = lax.axis_index("x") * lax.axis_size("zl") + lax.axis_index("zl")
    starts = (jnp.cumsum(doc_lengths) - doc_lengths - part * (slabs * tok_dev)).reshape(1, -1)
    starts = starts.astype(jnp.float32)

    keys = split_keys(section_token_rows, row_target, tp_count)
    keys = exchange(keys, "tp").reshape(tok_dev, KEY_CHUNK)
    keys, forward, backward = sort_rows(keys, parts, per_pair)
    load, places = arrange(exchange(keys, PART), per_pair)

    load, rows = lax.optimization_barrier((load, section_token_rows))
    queries = split_queries(rows, tp_count)
    queries = exchange(queries, "tp").reshape(tok_dev, QUERY_WIDTH)
    queries = permute_rows(forward, queries)
    queries = exchange(queries.reshape(parts, tok_dev // parts, QUERY_WIDTH), PART)
    queries = queries.reshape(parts, slabs, per_pair, QUERY_WIDTH).transpose(1, 0, 2, 3)
    queries = queries.reshape(tok_dev, QUERY_WIDTH)

    def passed(block, sign):
        route = []
        for at in range(slabs):
            for low in range(2):
                to = (at + sign * (1 - 2 * low)) % slabs
                route.append((at * 2 + low, to * 2 + low))
        return lax.ppermute(block, RING, route)

    loads = [load]
    load_a, load_b = load, load
    for _ in range(1, slabs // 2):
        load_a = passed(load_a, 1)
        load_b = passed(load_b, -1)
        loads += [load_a, load_b]
    last_keys = passed(load_a[:, :HEAD_SIZE], 1)
    last_values = passed(load_b[:, HEAD_SIZE:], -1)
    loads, values = loads + [last_keys], loads + [last_values]

    done = attend(starts, places, queries, loads, values, parts, per_pair)
    back = exchange(done, PART).reshape(tok_dev, QUERY_WIDTH)
    back = permute_rows(backward, back).reshape(tp_count, local_rows, QUERY_WIDTH)
    back = exchange(back, "tp")
    return back.transpose(1, 0, 2).reshape(local_rows, tp_count * QUERY_WIDTH)


def solution(mesh):
    shape = (4, 8, 2, mesh.shape["tp"])
    ring_mesh = Mesh(mesh.devices.reshape(shape), AXES)
    placed = (P(AXES, None), P(AXES), P())
    return jax.shard_map(
        per_device, mesh=ring_mesh, in_specs=placed, out_specs=P(AXES, None), check_vma=False
    )
```

```python
import functools
import math

import jax
import jax.numpy as jnp
from jax import lax
from jax.experimental import pallas as pl
from jax.experimental.pallas import tpu as pltpu
from jax.sharding import Mesh
from jax.sharding import PartitionSpec as P

HEAD_SIZE = 128
QUERY_PER_KEY = 5
LANES = 128
BLOCK = 512
QUERY_WIDTH = QUERY_PER_KEY * HEAD_SIZE
KV_WIDTH = 2 * HEAD_SIZE
MASKED = -1e30
VMEM_LIMIT = 24 * 1024 * 1024
AXES = ("x", "zh", "zl", "tp")
PART = ("x", "zl")
RING = ("zh", "zl")


def whole(n):
    return [pl.BlockSpec(memory_space=pltpu.VMEM)] * n


def params():
    return pltpu.CompilerParams(vmem_limit_bytes=VMEM_LIMIT)


def cost(flops, moved):
    return pl.CostEstimate(flops=flops, bytes_accessed=moved, transcendentals=0)


def iota(shape, axis):
    return lax.broadcasted_iota(jnp.int32, shape, axis)


def eye(n):
    return iota((n, n), 0) == iota((n, n), 1)


def column_to_row(column):
    n = column.shape[0]
    return jnp.sum(jnp.where(eye(n), column, 0.0), axis=0, keepdims=True)


def split_keys_kernel(target_ref, rows_ref, out_ref, target_at, coded_ref, sems):
    groups, _, _ = out_ref.shape
    n = rows_ref.shape[0]
    width = rows_ref.shape[1] // groups
    fetch = pltpu.make_async_copy(target_ref, target_at, sems.at[groups])
    fetch.start()
    copies = [
        pltpu.make_async_copy(
            rows_ref.at[:, pl.ds(g * width + QUERY_WIDTH, KV_WIDTH)],
            out_ref.at[g, pl.ds(0, n), :],
            sems.at[g],
        )
        for g in range(groups)
    ]
    for copy in copies:
        copy.start()
    coded_ref[...] = jnp.zeros_like(coded_ref)
    fetch.wait()
    coded_ref[0:1, 0:n] = (target_at[...] >> 8).astype(jnp.float32)
    coded_ref[1:2, 0:n] = (target_at[...] & 255).astype(jnp.float32)
    coded = coded_ref[...].astype(out_ref.dtype)
    for g in range(groups):
        out_ref[g, n:, :] = coded
    for copy in copies:
        copy.wait()


def split_keys(rows, target, groups):
    n = rows.shape[0]
    hbm = pl.BlockSpec(memory_space=pltpu.HBM)
    return pl.pallas_call(
        split_keys_kernel,
        in_specs=[hbm, hbm],
        out_specs=pl.BlockSpec(memory_space=pltpu.VMEM),
        out_shape=jax.ShapeDtypeStruct((groups, n + 8, KV_WIDTH), rows.dtype),
        scratch_shapes=[
            pltpu.VMEM((1, n), jnp.int32),
            pltpu.VMEM((8, KV_WIDTH), jnp.float32),
            pltpu.SemaphoreType.DMA((groups + 1,)),
        ],
        compiler_params=params(),
        cost_estimate=cost(0, 4 * groups * n * KV_WIDTH),
        name="split_keys",
    )(*[pltpu.with_memory_space_constraint(v, pltpu.HBM) for v in (target.reshape(1, n), rows)])


def split_queries_kernel(rows_ref, out_ref):
    out_ref[0] = rows_ref[:, :QUERY_WIDTH]


def split_queries(rows, groups):
    n, width = rows.shape
    return pl.pallas_call(
        split_queries_kernel,
        grid=(groups,),
        in_specs=[pl.BlockSpec((n, width // groups), lambda g: (0, g))],
        out_specs=pl.BlockSpec((1, n, QUERY_WIDTH), lambda g: (g, 0, 0)),
        out_shape=jax.ShapeDtypeStruct((groups, n, QUERY_WIDTH), rows.dtype),
        compiler_params=params(),
        cost_estimate=cost(0, 4 * rows.size),
        name="split_queries",
    )(rows)


def lanes_to_column(row, n):
    diagonal = iota((n, LANES), 0) == iota((n, LANES), 1)
    return jnp.sum(jnp.where(diagonal, row, 0.0), axis=1, keepdims=True)


def column_to_lanes(column):
    n = column.shape[0]
    diagonal = iota((n, LANES), 0) == iota((n, LANES), 1)
    return jnp.sum(jnp.where(diagonal, column, 0.0), axis=0, keepdims=True)


def sort_kernel(per_pair, chunk_ref, keys_ref, forward_ref, backward_ref):
    members, height, _ = chunk_ref.shape
    local_rows = height - 8
    n = members * local_rows
    parts = keys_ref.shape[0]
    padded = keys_ref.shape[1] - 8
    targets = []
    for m in range(members):
        coded = chunk_ref[m, local_rows:, :LANES].astype(jnp.float32)
        targets.append(lanes_to_column(coded[0:1] * 256.0 + coded[1:2], local_rows))
    column = jnp.concatenate(targets, axis=0)
    row = column_to_row(column)
    rank_row = jnp.sum(jnp.where(column < row, 1.0, 0.0), axis=0, keepdims=True)
    rank_column = jnp.sum(jnp.where(row < column, 1.0, 0.0), axis=1, keepdims=True)
    down = iota((n, n), 0).astype(jnp.float32)
    across = iota((n, n), 1).astype(jnp.float32)
    forward_ref[...] = jnp.where(rank_row == down, 1.0, 0.0).astype(jnp.bfloat16)
    backward_ref[...] = jnp.where(rank_column == across, 1.0, 0.0).astype(jnp.bfloat16)
    local = column - BLOCK * jnp.floor(column * (1.0 / BLOCK)) - BLOCK // 2
    tile = jnp.where(iota((n, LANES), 1) == 0, local, 0.0).astype(jnp.bfloat16)
    wanted = jnp.concatenate(
        [(iota((padded, n), 0) + (p * (n // parts) - per_pair)) & (n - 1) for p in range(parts)],
        axis=0,
    ).astype(jnp.float32)
    order = jnp.where(rank_row == wanted, 1.0, 0.0).astype(jnp.bfloat16)
    rows = jnp.concatenate([chunk_ref[m, :local_rows, :] for m in range(members)], axis=0)
    keys = jnp.dot(order, rows, preferred_element_type=jnp.float32)
    places = jnp.dot(order, tile, preferred_element_type=jnp.float32)[:, 0:1]
    for p in range(parts):
        at = slice(p * padded, (p + 1) * padded)
        place = jnp.where(iota((8, LANES), 0) == 0, column_to_lanes(places[at]), 0.0)
        place = jnp.concatenate([place, jnp.zeros_like(place)], axis=1)
        keys_ref[p] = jnp.concatenate([keys[at], place], axis=0).astype(keys_ref.dtype)


def sort_rows(chunk, parts, per_pair):
    members, height, width = chunk.shape
    n = members * (height - 8)
    padded = n // parts + per_pair
    return pl.pallas_call(
        functools.partial(sort_kernel, per_pair),
        in_specs=whole(1),
        out_specs=whole(3),
        out_shape=[
            jax.ShapeDtypeStruct((parts, padded + 8, width), chunk.dtype),
            jax.ShapeDtypeStruct((n, n), jnp.bfloat16),
            jax.ShapeDtypeStruct((n, n), jnp.bfloat16),
        ],
        compiler_params=params(),
        cost_estimate=cost(2 * n * chunk.size, 4 * chunk.size),
        name="sort_rows",
    )(chunk)


def permute_kernel(order_ref, chunk_ref, out_ref):
    out_ref[...] = jnp.dot(
        order_ref[...], chunk_ref[...], preferred_element_type=jnp.float32
    ).astype(out_ref.dtype)


def permute_rows(order, chunk):
    return pl.pallas_call(
        permute_kernel,
        in_specs=whole(2),
        out_specs=pl.BlockSpec(memory_space=pltpu.VMEM),
        out_shape=jax.ShapeDtypeStruct(chunk.shape, chunk.dtype),
        compiler_params=params(),
        cost_estimate=cost(2 * chunk.shape[0] * chunk.size, 4 * chunk.size),
    )(order, chunk)


def arrange_kernel(per_pair, got_ref, load_ref, place_ref):
    sources, height, _ = got_ref.shape
    padded = height - 8
    blocks = padded // per_pair
    span = sources * per_pair
    pieces = [got_ref[s].astype(jnp.float32) for s in range(sources)]
    columns = [lanes_to_column(piece[padded : padded + 1, :LANES], padded) for piece in pieces]
    places = []
    for b in range(blocks):
        rows = slice(b * per_pair, (b + 1) * per_pair)
        block = jnp.concatenate([piece[rows] for piece in pieces], axis=0)
        at = slice(b * span, (b + 1) * span)
        load_ref[at, :] = block.astype(load_ref.dtype)
        places.append(jnp.concatenate([column[rows] for column in columns], axis=0))
        place_ref[at, :] = jnp.broadcast_to(places[b], (span, LANES))
    rows = jnp.zeros((8, LANES), jnp.float32)
    for b in range(1, blocks):
        pair = jnp.concatenate([places[b - 1], places[b]], axis=0)
        rows = jnp.where(iota((8, LANES), 0) == b - 1, column_to_row(pair), rows)
    load_ref[blocks * span :, :HEAD_SIZE] = rows.astype(load_ref.dtype)
    load_ref[blocks * span :, HEAD_SIZE:] = jnp.zeros((8, HEAD_SIZE), load_ref.dtype)


def arrange(got, per_pair):
    sources, height, _ = got.shape
    rows = sources * (height - 8)
    return pl.pallas_call(
        functools.partial(arrange_kernel, per_pair),
        in_specs=whole(1),
        out_specs=whole(2),
        out_shape=[
            jax.ShapeDtypeStruct((rows + 8, KV_WIDTH), got.dtype),
            jax.ShapeDtypeStruct((rows, LANES), jnp.float32),
        ],
        compiler_params=params(),
        cost_estimate=cost(0, 4 * got.size),
        name="arrange",
    )(got)


def attend_kernel(per_pair, loads, last, starts_ref, place_ref, query_ref, *refs):
    load_refs, value_refs, refs = refs[:loads], refs[loads : 2 * loads], refs[2 * loads :]
    if last:
        before_ref, stats_ref, out_ref, key_ref, value_ref, done_ref = refs
    else:
        done_ref, stats_ref, key_ref, value_ref = refs
    n = query_ref.shape[0]
    heads = QUERY_PER_KEY
    span = place_ref.shape[0] - n
    sources = span // per_pair
    blocks = n // span
    pair = 2 * span
    keys = loads * pair
    scale = math.log2(math.e) / math.sqrt(HEAD_SIZE)
    half = float(BLOCK // 2)
    lane = iota((1, pair), 1)
    shift = jnp.where(lane < span, half - BLOCK, half)
    starts = starts_ref[...]
    for b in range(blocks):
        rows = slice(b * span, b * span + pair)
        for at in range(loads):
            key_ref[at * pair : (at + 1) * pair, :] = load_refs[at][rows, :HEAD_SIZE]
            value_ref[at * pair : (at + 1) * pair, :] = value_refs[at][rows, -HEAD_SIZE:]
        key_place = jnp.concatenate(
            [
                load_ref[(blocks + 1) * span :, :LANES].astype(jnp.float32)[b : b + 1] + shift
                for load_ref in load_refs
            ],
            axis=1,
        )
        place = place_ref[(b + 1) * span : (b + 2) * span, 0:1] + half
        base = float(b * BLOCK)
        start = jnp.max(
            jnp.where(starts <= place + base, starts, -1e9), axis=1, keepdims=True
        )
        allowed = (key_place >= start - base) & (key_place <= place)
        bias = jnp.where(allowed, 0.0, MASKED)
        query = query_ref[b * span : (b + 1) * span, :]
        query = jnp.concatenate(
            [query[:, h * HEAD_SIZE : (h + 1) * HEAD_SIZE] for h in range(heads)], axis=0
        )
        scores = lax.dot_general(
            query, key_ref[...], (((1,), (1,)), ((), ())), preferred_element_type=jnp.float32
        )
        scores = scores.reshape(heads, span, keys) * scale + bias[None]
        scores = scores.reshape(heads * span, keys)
        top = jnp.max(scores, axis=1, keepdims=True)
        here = slice(b * heads * span, (b + 1) * heads * span)
        if last:
            stats = stats_ref[here, :]
            top_before, total_before = stats[:, 0:1], stats[:, LANES // 2 : LANES // 2 + 1]
            top = jnp.maximum(top, top_before)
        weights = jnp.exp2(scores - top)
        total = jnp.sum(weights, axis=1, keepdims=True)
        done = jnp.dot(
            weights.astype(jnp.bfloat16), value_ref[...], preferred_element_type=jnp.float32
        )
        if not last:
            done_ref[here, :] = done
            stats_ref[here, :] = jnp.where(
                iota((heads * span, LANES), 1) < LANES // 2, top, total
            )
            continue
        kept = jnp.exp2(top_before - top)
        done = (before_ref[here, :] * kept + done) / (total_before * kept + total)
        for h in range(heads):
            for s in range(sources):
                first = h * span + s * per_pair
                done_ref[
                    s, b * per_pair : (b + 1) * per_pair, h * HEAD_SIZE : (h + 1) * HEAD_SIZE
                ] = done[first : first + per_pair]
    if last:
        out_ref[...] = done_ref[...].astype(out_ref.dtype)


def attend(starts, places, queries, loads, values, sources, per_pair, before=()):
    n = queries.shape[0]
    keys = len(loads) * 2 * sources * per_pair
    flat = jax.ShapeDtypeStruct((n * QUERY_PER_KEY, HEAD_SIZE), jnp.float32)
    shape = (sources, n // sources, QUERY_WIDTH)
    last = bool(before)
    scratch = [pltpu.VMEM((keys, HEAD_SIZE), queries.dtype)] * 2
    return pl.pallas_call(
        functools.partial(attend_kernel, per_pair, len(loads), last),
        in_specs=whole(3 + 2 * len(loads) + len(before)),
        out_specs=whole(1)[0] if last else whole(2),
        out_shape=jax.ShapeDtypeStruct(shape, queries.dtype) if last else [flat, flat],
        scratch_shapes=scratch + ([pltpu.VMEM(shape, jnp.float32)] if last else []),
        compiler_params=params(),
        cost_estimate=cost(4 * n * keys * QUERY_WIDTH, 4 * n * QUERY_WIDTH),
        name="attend_last" if last else "attend_most",
    )(starts, places, queries, *loads, *values, *before)


def exchange(blocks, axis):
    return lax.all_to_all(blocks, axis, split_axis=0, concat_axis=0, tiled=True)


def per_device(section_token_rows, row_target, doc_lengths):
    tp_count = lax.axis_size("tp")
    slabs = lax.axis_size("zh")
    parts = lax.axis_size("x") * lax.axis_size("zl")
    local_rows = section_token_rows.shape[0]
    tok_dev = local_rows * tp_count
    per_pair = tok_dev // (parts * slabs)
    part = lax.axis_index("x") * lax.axis_size("zl") + lax.axis_index("zl")
    starts = (jnp.cumsum(doc_lengths) - doc_lengths - part * (slabs * tok_dev)).reshape(1, -1)
    starts = starts.astype(jnp.float32)

    keys = split_keys(section_token_rows, row_target, tp_count)
    keys = exchange(keys, "tp")
    keys, forward, backward = sort_rows(keys, parts, per_pair)
    load, places = arrange(exchange(keys, PART), per_pair)

    load, rows = lax.optimization_barrier((load, section_token_rows))
    queries = split_queries(rows, tp_count)
    queries = exchange(queries, "tp").reshape(tok_dev, QUERY_WIDTH)
    queries = permute_rows(forward, queries)
    queries = exchange(queries.reshape(parts, tok_dev // parts, QUERY_WIDTH), PART)
    queries = queries.reshape(parts, slabs, per_pair, QUERY_WIDTH).transpose(1, 0, 2, 3)
    queries = queries.reshape(tok_dev, QUERY_WIDTH)

    def passed(block, sign):
        route = []
        for at in range(slabs):
            for low in range(2):
                to = (at + sign * (1 - 2 * low)) % slabs
                route.append((at * 2 + low, to * 2 + low))
        return lax.ppermute(block, RING, route)

    loads = [load]
    load_a, load_b = load, load
    for _ in range(1, slabs // 2):
        load_a = passed(load_a, 1)
        load_b = passed(load_b, -1)
        loads += [load_a, load_b]
    last_keys = passed(load_a[:, :HEAD_SIZE], 1)
    last_values = passed(load_b[:, HEAD_SIZE:], -1)

    before = attend(starts, places, queries, loads, loads, parts, per_pair)
    done = attend(
        starts, places, queries, [last_keys], [last_values], parts, per_pair, before
    )
    back = exchange(done, PART).reshape(tok_dev, QUERY_WIDTH)
    back = permute_rows(backward, back).reshape(tp_count, local_rows, QUERY_WIDTH)
    back = exchange(back, "tp")
    return back.transpose(1, 0, 2).reshape(local_rows, tp_count * QUERY_WIDTH)


def solution(mesh):
    shape = (4, 8, 2, mesh.shape["tp"])
    ring_mesh = Mesh(mesh.devices.reshape(shape), AXES)
    placed = (P(AXES, None), P(AXES), P())
    return jax.shard_map(
        per_device, mesh=ring_mesh, in_specs=placed, out_specs=P(AXES, None), check_vma=False
    )
```

```python
import functools
import math

import jax
import jax.numpy as jnp
from jax import lax
from jax.experimental import pallas as pl
from jax.experimental.pallas import tpu as pltpu
from jax.sharding import Mesh
from jax.sharding import PartitionSpec as P

HEAD_SIZE = 128
QUERY_PER_KEY = 5
LANES = 128
BLOCK = 512
QUERY_WIDTH = QUERY_PER_KEY * HEAD_SIZE
KV_WIDTH = 2 * HEAD_SIZE
MASKED = -1e30
VMEM_LIMIT = 24 * 1024 * 1024
AXES = ("x", "zh", "zl", "tp")
PART = ("x", "zl")
RING = ("zh", "zl")


def whole(n):
    return [pl.BlockSpec(memory_space=pltpu.VMEM)] * n


def params():
    return pltpu.CompilerParams(vmem_limit_bytes=VMEM_LIMIT)


def cost(flops, moved):
    return pl.CostEstimate(flops=flops, bytes_accessed=moved, transcendentals=0)


def iota(shape, axis):
    return lax.broadcasted_iota(jnp.int32, shape, axis)


def eye(n):
    return iota((n, n), 0) == iota((n, n), 1)


def column_to_row(column):
    n = column.shape[0]
    return jnp.sum(jnp.where(eye(n), column, 0.0), axis=0, keepdims=True)


def split_keys_kernel(target_ref, rows_ref, out_ref, target_at, coded_ref, sems):
    groups, _, _ = out_ref.shape
    n = rows_ref.shape[0]
    width = rows_ref.shape[1] // groups
    fetch = pltpu.make_async_copy(target_ref, target_at, sems.at[groups])
    fetch.start()
    copies = [
        pltpu.make_async_copy(
            rows_ref.at[:, pl.ds(g * width + QUERY_WIDTH, KV_WIDTH)],
            out_ref.at[g, pl.ds(0, n), :],
            sems.at[g],
        )
        for g in range(groups)
    ]
    for copy in copies:
        copy.start()
    coded_ref[...] = jnp.zeros_like(coded_ref)
    fetch.wait()
    coded_ref[0:1, 0:n] = (target_at[...] >> 8).astype(jnp.float32)
    coded_ref[1:2, 0:n] = (target_at[...] & 255).astype(jnp.float32)
    coded = coded_ref[...].astype(out_ref.dtype)
    for g in range(groups):
        out_ref[g, n:, :] = coded
    for copy in copies:
        copy.wait()


def split_keys(rows, target, groups):
    n = rows.shape[0]
    hbm = pl.BlockSpec(memory_space=pltpu.HBM)
    return pl.pallas_call(
        split_keys_kernel,
        in_specs=[hbm, hbm],
        out_specs=pl.BlockSpec(memory_space=pltpu.VMEM),
        out_shape=jax.ShapeDtypeStruct((groups, n + 8, KV_WIDTH), rows.dtype),
        scratch_shapes=[
            pltpu.VMEM((1, n), jnp.int32),
            pltpu.VMEM((8, KV_WIDTH), jnp.float32),
            pltpu.SemaphoreType.DMA((groups + 1,)),
        ],
        compiler_params=params(),
        cost_estimate=cost(0, 4 * groups * n * KV_WIDTH),
        name="split_keys",
    )(*[pltpu.with_memory_space_constraint(v, pltpu.HBM) for v in (target.reshape(1, n), rows)])


def split_queries_kernel(rows_ref, out_ref):
    out_ref[0] = rows_ref[:, :QUERY_WIDTH]


def split_queries(rows, groups):
    n, width = rows.shape
    return pl.pallas_call(
        split_queries_kernel,
        grid=(groups,),
        in_specs=[pl.BlockSpec((n, width // groups), lambda g: (0, g))],
        out_specs=pl.BlockSpec((1, n, QUERY_WIDTH), lambda g: (g, 0, 0)),
        out_shape=jax.ShapeDtypeStruct((groups, n, QUERY_WIDTH), rows.dtype),
        compiler_params=params(),
        cost_estimate=cost(0, 4 * rows.size),
        name="split_queries",
    )(rows)


def lanes_to_column(row, n):
    diagonal = iota((n, LANES), 0) == iota((n, LANES), 1)
    return jnp.sum(jnp.where(diagonal, row, 0.0), axis=1, keepdims=True)


def column_to_lanes(column):
    n = column.shape[0]
    diagonal = iota((n, LANES), 0) == iota((n, LANES), 1)
    return jnp.sum(jnp.where(diagonal, column, 0.0), axis=0, keepdims=True)


def sort_kernel(per_pair, chunk_ref, keys_ref, forward_ref, backward_ref):
    members, height, _ = chunk_ref.shape
    local_rows = height - 8
    n = members * local_rows
    parts = keys_ref.shape[0]
    padded = keys_ref.shape[1] - 8
    targets = []
    for m in range(members):
        coded = chunk_ref[m, local_rows:, :LANES].astype(jnp.float32)
        targets.append(lanes_to_column(coded[0:1] * 256.0 + coded[1:2], local_rows))
    column = jnp.concatenate(targets, axis=0)
    row = column_to_row(column)
    rank_row = jnp.sum(jnp.where(column < row, 1.0, 0.0), axis=0, keepdims=True)
    rank_column = jnp.sum(jnp.where(row < column, 1.0, 0.0), axis=1, keepdims=True)
    down = iota((n, n), 0).astype(jnp.float32)
    across = iota((n, n), 1).astype(jnp.float32)
    forward_ref[...] = jnp.where(rank_row == down, 1.0, 0.0).astype(jnp.bfloat16)
    backward_ref[...] = jnp.where(rank_column == across, 1.0, 0.0).astype(jnp.bfloat16)
    local = column - BLOCK * jnp.floor(column * (1.0 / BLOCK)) - BLOCK // 2
    tile = jnp.where(iota((n, LANES), 1) == 0, local, 0.0).astype(jnp.bfloat16)
    wanted = jnp.concatenate(
        [(iota((padded, n), 0) + (p * (n // parts) - per_pair)) & (n - 1) for p in range(parts)],
        axis=0,
    ).astype(jnp.float32)
    order = jnp.where(rank_row == wanted, 1.0, 0.0).astype(jnp.bfloat16)
    rows = jnp.concatenate([chunk_ref[m, :local_rows, :] for m in range(members)], axis=0)
    keys = jnp.dot(order, rows, preferred_element_type=jnp.float32)
    places = jnp.dot(order, tile, preferred_element_type=jnp.float32)[:, 0:1]
    for p in range(parts):
        at = slice(p * padded, (p + 1) * padded)
        place = jnp.where(iota((8, LANES), 0) == 0, column_to_lanes(places[at]), 0.0)
        place = jnp.concatenate([place, jnp.zeros_like(place)], axis=1)
        keys_ref[p] = jnp.concatenate([keys[at], place], axis=0).astype(keys_ref.dtype)


def sort_rows(chunk, parts, per_pair):
    members, height, width = chunk.shape
    n = members * (height - 8)
    padded = n // parts + per_pair
    return pl.pallas_call(
        functools.partial(sort_kernel, per_pair),
        in_specs=whole(1),
        out_specs=whole(3),
        out_shape=[
            jax.ShapeDtypeStruct((parts, padded + 8, width), chunk.dtype),
            jax.ShapeDtypeStruct((n, n), jnp.bfloat16),
            jax.ShapeDtypeStruct((n, n), jnp.bfloat16),
        ],
        compiler_params=params(),
        cost_estimate=cost(2 * n * chunk.size, 4 * chunk.size),
        name="sort_rows",
    )(chunk)


def permute_kernel(order_ref, chunk_ref, out_ref):
    out_ref[...] = jnp.dot(
        order_ref[...], chunk_ref[...], preferred_element_type=jnp.float32
    ).astype(out_ref.dtype)


def permute_rows(order, chunk):
    return pl.pallas_call(
        permute_kernel,
        in_specs=whole(2),
        out_specs=pl.BlockSpec(memory_space=pltpu.VMEM),
        out_shape=jax.ShapeDtypeStruct(chunk.shape, chunk.dtype),
        compiler_params=params(),
        cost_estimate=cost(2 * chunk.shape[0] * chunk.size, 4 * chunk.size),
    )(order, chunk)


def arrange_kernel(per_pair, got_ref, load_ref, place_ref):
    sources, height, _ = got_ref.shape
    padded = height - 8
    blocks = padded // per_pair
    span = sources * per_pair
    pieces = [got_ref[s].astype(jnp.float32) for s in range(sources)]
    columns = [lanes_to_column(piece[padded : padded + 1, :LANES], padded) for piece in pieces]
    places = []
    for b in range(blocks):
        rows = slice(b * per_pair, (b + 1) * per_pair)
        block = jnp.concatenate([piece[rows] for piece in pieces], axis=0)
        at = slice(b * span, (b + 1) * span)
        load_ref[at, :] = block.astype(load_ref.dtype)
        places.append(jnp.concatenate([column[rows] for column in columns], axis=0))
        place_ref[at, :] = jnp.broadcast_to(places[b], (span, LANES))
    rows = jnp.zeros((8, LANES), jnp.float32)
    for b in range(1, blocks):
        pair = jnp.concatenate([places[b - 1], places[b]], axis=0)
        rows = jnp.where(iota((8, LANES), 0) == b - 1, column_to_row(pair), rows)
    load_ref[blocks * span :, :HEAD_SIZE] = rows.astype(load_ref.dtype)
    load_ref[blocks * span :, HEAD_SIZE:] = jnp.zeros((8, HEAD_SIZE), load_ref.dtype)


def arrange(got, per_pair):
    sources, height, _ = got.shape
    rows = sources * (height - 8)
    return pl.pallas_call(
        functools.partial(arrange_kernel, per_pair),
        in_specs=whole(1),
        out_specs=whole(2),
        out_shape=[
            jax.ShapeDtypeStruct((rows + 8, KV_WIDTH), got.dtype),
            jax.ShapeDtypeStruct((rows, LANES), jnp.float32),
        ],
        compiler_params=params(),
        cost_estimate=cost(0, 4 * got.size),
        name="arrange",
    )(got)


def attend_kernel(per_pair, loads, starts_ref, place_ref, query_ref, *refs):
    load_refs, value_refs = refs[:loads], refs[loads : 2 * loads]
    out_ref, key_ref, value_ref, done_ref = refs[2 * loads :]
    sources = out_ref.shape[0]
    span = sources * per_pair
    blocks = out_ref.shape[1] // per_pair
    pair = 2 * span
    scale = math.log2(math.e) / math.sqrt(HEAD_SIZE)
    half = float(BLOCK // 2)
    lane = iota((1, pair), 1)
    shift = jnp.where(lane < span, half - BLOCK, half)
    starts = starts_ref[...]
    for b in range(blocks):
        rows = slice(b * span, b * span + pair)
        for at in range(loads):
            key_ref[at * pair : (at + 1) * pair, :] = load_refs[at][rows, :HEAD_SIZE]
            value_ref[at * pair : (at + 1) * pair, :] = value_refs[at][rows, -HEAD_SIZE:]
        key_place = jnp.concatenate(
            [
                load_ref[(blocks + 1) * span :, :LANES].astype(jnp.float32)[b : b + 1] + shift
                for load_ref in load_refs
            ],
            axis=1,
        )
        place = place_ref[(b + 1) * span : (b + 2) * span, 0:1] + half
        base = float(b * BLOCK)
        start = jnp.max(
            jnp.where(starts <= place + base, starts, -1e9), axis=1, keepdims=True
        )
        allowed = (key_place >= start - base) & (key_place <= place)
        bias = jnp.where(allowed, 0.0, MASKED)
        query = query_ref[b * span : (b + 1) * span, :]
        query = jnp.concatenate(
            [query[:, h * HEAD_SIZE : (h + 1) * HEAD_SIZE] for h in range(QUERY_PER_KEY)], axis=0
        )
        scores = lax.dot_general(
            query, key_ref[...], (((1,), (1,)), ((), ())), preferred_element_type=jnp.float32
        )
        scores = scores.reshape(QUERY_PER_KEY, span, loads * pair) * scale + bias[None]
        weights = jnp.exp2(scores - jnp.max(scores, axis=2, keepdims=True))
        total = jnp.sum(weights, axis=2, keepdims=True).reshape(QUERY_PER_KEY * span, 1)
        weights = weights.astype(jnp.bfloat16).reshape(QUERY_PER_KEY * span, loads * pair)
        done = jnp.dot(weights, value_ref[...], preferred_element_type=jnp.float32) / total
        for h in range(QUERY_PER_KEY):
            for s in range(sources):
                first = h * span + s * per_pair
                done_ref[
                    s, b * per_pair : (b + 1) * per_pair, h * HEAD_SIZE : (h + 1) * HEAD_SIZE
                ] = done[first : first + per_pair]
    out_ref[...] = done_ref[...].astype(out_ref.dtype)


def attend(starts, places, queries, loads, values, sources, per_pair):
    n = queries.shape[0]
    keys = len(loads) * 2 * sources * per_pair
    shape = (sources, n // sources, QUERY_WIDTH)
    return pl.pallas_call(
        functools.partial(attend_kernel, per_pair, len(loads)),
        in_specs=whole(3 + 2 * len(loads)),
        out_specs=pl.BlockSpec(memory_space=pltpu.VMEM),
        out_shape=jax.ShapeDtypeStruct(shape, queries.dtype),
        scratch_shapes=[
            pltpu.VMEM((keys, HEAD_SIZE), queries.dtype),
            pltpu.VMEM((keys, HEAD_SIZE), queries.dtype),
            pltpu.VMEM(shape, jnp.float32),
        ],
        compiler_params=params(),
        cost_estimate=cost(4 * n * keys * QUERY_WIDTH, 4 * n * QUERY_WIDTH),
        name="attend",
    )(starts, places, queries, *loads, *values)


def exchange(blocks, axis):
    return lax.all_to_all(blocks, axis, split_axis=0, concat_axis=0, tiled=True)


def per_device(section_token_rows, row_target, doc_lengths):
    tp_count = lax.axis_size("tp")
    slabs = lax.axis_size("zh")
    parts = lax.axis_size("x") * lax.axis_size("zl")
    local_rows = section_token_rows.shape[0]
    tok_dev = local_rows * tp_count
    per_pair = tok_dev // (parts * slabs)
    part = lax.axis_index("x") * lax.axis_size("zl") + lax.axis_index("zl")
    starts = (jnp.cumsum(doc_lengths) - doc_lengths - part * (slabs * tok_dev)).reshape(1, -1)
    starts = starts.astype(jnp.float32)

    keys = split_keys(section_token_rows, row_target, tp_count)
    keys = exchange(keys, "tp")
    keys, forward, backward = sort_rows(keys, parts, per_pair)
    load, places = arrange(exchange(keys, PART), per_pair)

    load, rows = lax.optimization_barrier((load, section_token_rows))
    queries = split_queries(rows, tp_count)
    queries = exchange(queries, "tp").reshape(tok_dev, QUERY_WIDTH)
    queries = permute_rows(forward, queries)
    queries = exchange(queries.reshape(parts, tok_dev // parts, QUERY_WIDTH), PART)
    queries = queries.reshape(parts, slabs, per_pair, QUERY_WIDTH).transpose(1, 0, 2, 3)
    queries = queries.reshape(tok_dev, QUERY_WIDTH)

    def passed(block, sign):
        route = []
        for at in range(slabs):
            for low in range(2):
                to = (at + sign * (1 - 2 * low)) % slabs
                route.append((at * 2 + low, to * 2 + low))
        return lax.ppermute(block, RING, route)

    loads = [load]
    load_a, load_b = load, load
    for _ in range(1, slabs // 2):
        load_a = passed(load_a, 1)
        load_b = passed(load_b, -1)
        loads += [load_a, load_b]
    last_keys = passed(load_a[:, :HEAD_SIZE], 1)
    last_values = passed(load_b[:, HEAD_SIZE:], -1)
    loads, values = loads + [last_keys], loads + [last_values]

    done = attend(starts, places, queries, loads, values, parts, per_pair)
    back = exchange(done, PART).reshape(tok_dev, QUERY_WIDTH)
    back = permute_rows(backward, back).reshape(tp_count, local_rows, QUERY_WIDTH)
    back = exchange(back, "tp")
    return back.transpose(1, 0, 2).reshape(local_rows, tp_count * QUERY_WIDTH)


def solution(mesh):
    shape = (4, 8, 2, mesh.shape["tp"])
    ring_mesh = Mesh(mesh.devices.reshape(shape), AXES)
    placed = (P(AXES, None), P(AXES), P())
    return jax.shard_map(
        per_device, mesh=ring_mesh, in_specs=placed, out_specs=P(AXES, None), check_vma=False
    )
```

```python
import functools
import math

import jax
import jax.numpy as jnp
from jax import lax
from jax.experimental import pallas as pl
from jax.experimental.pallas import tpu as pltpu
from jax.sharding import Mesh
from jax.sharding import PartitionSpec as P

HEAD_SIZE = 128
QUERY_PER_KEY = 5
LANES = 128
BLOCK = 512
QUERY_WIDTH = QUERY_PER_KEY * HEAD_SIZE
KV_WIDTH = 2 * HEAD_SIZE
MASKED = -1e30
VMEM_LIMIT = 24 * 1024 * 1024
AXES = ("x", "zh", "zl", "tp")
PART = ("x", "zl")
RING = ("zh", "zl")


def whole(n):
    return [pl.BlockSpec(memory_space=pltpu.VMEM)] * n


def params():
    return pltpu.CompilerParams(vmem_limit_bytes=VMEM_LIMIT)


def cost(flops, moved):
    return pl.CostEstimate(flops=flops, bytes_accessed=moved, transcendentals=0)


def iota(shape, axis):
    return lax.broadcasted_iota(jnp.int32, shape, axis)


def eye(n):
    return iota((n, n), 0) == iota((n, n), 1)


def column_to_row(column):
    n = column.shape[0]
    return jnp.sum(jnp.where(eye(n), column, 0.0), axis=0, keepdims=True)


def split_keys_kernel(target_ref, rows_ref, out_ref, target_at, coded_ref, sems):
    groups, _, _ = out_ref.shape
    n = rows_ref.shape[0]
    width = rows_ref.shape[1] // groups
    fetch = pltpu.make_async_copy(target_ref, target_at, sems.at[groups])
    fetch.start()
    copies = [
        pltpu.make_async_copy(
            rows_ref.at[:, pl.ds(g * width + QUERY_WIDTH, KV_WIDTH)],
            out_ref.at[g, pl.ds(0, n), :],
            sems.at[g],
        )
        for g in range(groups)
    ]
    for copy in copies:
        copy.start()
    coded_ref[...] = jnp.zeros_like(coded_ref)
    fetch.wait()
    coded_ref[0:1, 0:n] = (target_at[...] >> 8).astype(jnp.float32)
    coded_ref[1:2, 0:n] = (target_at[...] & 255).astype(jnp.float32)
    coded = coded_ref[...].astype(out_ref.dtype)
    for g in range(groups):
        out_ref[g, n:, :] = coded
    for copy in copies:
        copy.wait()


def split_keys(rows, target, groups):
    n = rows.shape[0]
    hbm = pl.BlockSpec(memory_space=pltpu.HBM)
    return pl.pallas_call(
        split_keys_kernel,
        in_specs=[hbm, hbm],
        out_specs=pl.BlockSpec(memory_space=pltpu.VMEM),
        out_shape=jax.ShapeDtypeStruct((groups, n + 8, KV_WIDTH), rows.dtype),
        scratch_shapes=[
            pltpu.VMEM((1, n), jnp.int32),
            pltpu.VMEM((8, KV_WIDTH), jnp.float32),
            pltpu.SemaphoreType.DMA((groups + 1,)),
        ],
        compiler_params=params(),
        cost_estimate=cost(0, 4 * groups * n * KV_WIDTH),
        name="split_keys",
    )(*[pltpu.with_memory_space_constraint(v, pltpu.HBM) for v in (target.reshape(1, n), rows)])


def split_queries_kernel(rows_ref, out_ref):
    out_ref[0] = rows_ref[:, :QUERY_WIDTH]


def split_queries(rows, groups):
    n, width = rows.shape
    return pl.pallas_call(
        split_queries_kernel,
        grid=(groups,),
        in_specs=[pl.BlockSpec((n, width // groups), lambda g: (0, g))],
        out_specs=pl.BlockSpec((1, n, QUERY_WIDTH), lambda g: (g, 0, 0)),
        out_shape=jax.ShapeDtypeStruct((groups, n, QUERY_WIDTH), rows.dtype),
        compiler_params=params(),
        cost_estimate=cost(0, 4 * rows.size),
        name="split_queries",
    )(rows)


def lanes_to_column(row, n):
    diagonal = iota((n, LANES), 0) == iota((n, LANES), 1)
    return jnp.sum(jnp.where(diagonal, row, 0.0), axis=1, keepdims=True)


def column_to_lanes(column):
    n = column.shape[0]
    diagonal = iota((n, LANES), 0) == iota((n, LANES), 1)
    return jnp.sum(jnp.where(diagonal, column, 0.0), axis=0, keepdims=True)


def sort_kernel(per_pair, chunk_ref, keys_ref, forward_ref, backward_ref):
    members, height, _ = chunk_ref.shape
    local_rows = height - 8
    n = members * local_rows
    parts = keys_ref.shape[0]
    padded = keys_ref.shape[1] - 8
    targets = []
    for m in range(members):
        coded = chunk_ref[m, local_rows:, :LANES].astype(jnp.float32)
        targets.append(lanes_to_column(coded[0:1] * 256.0 + coded[1:2], local_rows))
    column = jnp.concatenate(targets, axis=0)
    row = column_to_row(column)
    rank_row = jnp.sum(jnp.where(column < row, 1.0, 0.0), axis=0, keepdims=True)
    rank_column = jnp.sum(jnp.where(row < column, 1.0, 0.0), axis=1, keepdims=True)
    down = iota((n, n), 0).astype(jnp.float32)
    across = iota((n, n), 1).astype(jnp.float32)
    forward_ref[...] = jnp.where(rank_row == down, 1.0, 0.0).astype(jnp.bfloat16)
    backward_ref[...] = jnp.where(rank_column == across, 1.0, 0.0).astype(jnp.bfloat16)
    local = column - BLOCK * jnp.floor(column * (1.0 / BLOCK)) - BLOCK // 2
    tile = jnp.where(iota((n, LANES), 1) == 0, local, 0.0).astype(jnp.bfloat16)
    wanted = jnp.concatenate(
        [(iota((padded, n), 0) + (p * (n // parts) - per_pair)) & (n - 1) for p in range(parts)],
        axis=0,
    ).astype(jnp.float32)
    order = jnp.where(rank_row == wanted, 1.0, 0.0).astype(jnp.bfloat16)
    rows = jnp.concatenate([chunk_ref[m, :local_rows, :] for m in range(members)], axis=0)
    keys = jnp.dot(order, rows, preferred_element_type=jnp.float32)
    places = jnp.dot(order, tile, preferred_element_type=jnp.float32)[:, 0:1]
    for p in range(parts):
        at = slice(p * padded, (p + 1) * padded)
        place = jnp.where(iota((8, LANES), 0) == 0, column_to_lanes(places[at]), 0.0)
        place = jnp.concatenate([place, jnp.zeros_like(place)], axis=1)
        keys_ref[p] = jnp.concatenate([keys[at], place], axis=0).astype(keys_ref.dtype)


def sort_rows(chunk, parts, per_pair):
    members, height, width = chunk.shape
    n = members * (height - 8)
    padded = n // parts + per_pair
    return pl.pallas_call(
        functools.partial(sort_kernel, per_pair),
        in_specs=whole(1),
        out_specs=whole(3),
        out_shape=[
            jax.ShapeDtypeStruct((parts, padded + 8, width), chunk.dtype),
            jax.ShapeDtypeStruct((n, n), jnp.bfloat16),
            jax.ShapeDtypeStruct((n, n), jnp.bfloat16),
        ],
        compiler_params=params(),
        cost_estimate=cost(2 * n * chunk.size, 4 * chunk.size),
        name="sort_rows",
    )(chunk)


def permute_kernel(order_ref, chunk_ref, out_ref):
    out_ref[...] = jnp.dot(
        order_ref[...], chunk_ref[...], preferred_element_type=jnp.float32
    ).astype(out_ref.dtype)


def permute_rows(order, chunk):
    return pl.pallas_call(
        permute_kernel,
        in_specs=whole(2),
        out_specs=pl.BlockSpec(memory_space=pltpu.VMEM),
        out_shape=jax.ShapeDtypeStruct(chunk.shape, chunk.dtype),
        compiler_params=params(),
        cost_estimate=cost(2 * chunk.shape[0] * chunk.size, 4 * chunk.size),
    )(order, chunk)


def arrange_kernel(per_pair, got_ref, load_ref):
    sources, height, _ = got_ref.shape
    padded = height - 8
    blocks = padded // per_pair
    span = sources * per_pair
    pieces = [got_ref[s].astype(jnp.float32) for s in range(sources)]
    columns = [lanes_to_column(piece[padded : padded + 1, :LANES], padded) for piece in pieces]
    places = []
    for b in range(blocks):
        rows = slice(b * per_pair, (b + 1) * per_pair)
        block = jnp.concatenate([piece[rows] for piece in pieces], axis=0)
        at = slice(b * span, (b + 1) * span)
        load_ref[at, :] = block.astype(load_ref.dtype)
        places.append(jnp.concatenate([column[rows] for column in columns], axis=0))
    rows = jnp.zeros((8, LANES), jnp.float32)
    for b in range(1, blocks):
        pair = jnp.concatenate([places[b - 1], places[b]], axis=0)
        rows = jnp.where(iota((8, LANES), 0) == b - 1, column_to_row(pair), rows)
    load_ref[blocks * span :, :HEAD_SIZE] = rows.astype(load_ref.dtype)
    load_ref[blocks * span :, HEAD_SIZE:] = jnp.zeros((8, HEAD_SIZE), load_ref.dtype)


def arrange(got, per_pair):
    sources, height, _ = got.shape
    rows = sources * (height - 8)
    return pl.pallas_call(
        functools.partial(arrange_kernel, per_pair),
        in_specs=whole(1),
        out_specs=whole(1)[0],
        out_shape=jax.ShapeDtypeStruct((rows + 8, KV_WIDTH), got.dtype),
        compiler_params=params(),
        cost_estimate=cost(0, 4 * got.size),
        name="arrange",
    )(got)


def attend_kernel(per_pair, loads, starts_ref, query_ref, *refs):
    load_refs, value_refs = refs[:loads], refs[loads : 2 * loads]
    out_ref, key_ref, value_ref, done_ref = refs[2 * loads :]
    sources = out_ref.shape[0]
    span = sources * per_pair
    blocks = out_ref.shape[1] // per_pair
    pair = 2 * span
    scale = math.log2(math.e) / math.sqrt(HEAD_SIZE)
    half = float(BLOCK // 2)
    lane = iota((1, pair), 1)
    shift = jnp.where(lane < span, half - BLOCK, half)
    own_lane = iota((span, pair), 1) == iota((span, pair), 0) + span
    starts = starts_ref[...]
    for b in range(blocks):
        rows = slice(b * span, b * span + pair)
        for at in range(loads):
            key_ref[at * pair : (at + 1) * pair, :] = load_refs[at][rows, :HEAD_SIZE]
            value_ref[at * pair : (at + 1) * pair, :] = value_refs[at][rows, -HEAD_SIZE:]
        key_place = jnp.concatenate(
            [
                load_ref[(blocks + 1) * span :, :LANES].astype(jnp.float32)[b : b + 1] + shift
                for load_ref in load_refs
            ],
            axis=1,
        )
        place = jnp.where(own_lane, key_place[:, :pair], 0.0)
        place = jnp.sum(place, axis=1, keepdims=True)
        base = float(b * BLOCK)
        start = jnp.max(
            jnp.where(starts <= place + base, starts, -1e9), axis=1, keepdims=True
        )
        allowed = (key_place >= start - base) & (key_place <= place)
        bias = jnp.where(allowed, 0.0, MASKED)
        query = query_ref[b * span : (b + 1) * span, :]
        query = jnp.concatenate(
            [query[:, h * HEAD_SIZE : (h + 1) * HEAD_SIZE] for h in range(QUERY_PER_KEY)], axis=0
        )
        scores = lax.dot_general(
            query, key_ref[...], (((1,), (1,)), ((), ())), preferred_element_type=jnp.float32
        )
        scores = scores.reshape(QUERY_PER_KEY, span, loads * pair) * scale + bias[None]
        weights = jnp.exp2(scores - jnp.max(scores, axis=2, keepdims=True))
        total = jnp.sum(weights, axis=2, keepdims=True).reshape(QUERY_PER_KEY * span, 1)
        weights = weights.astype(jnp.bfloat16).reshape(QUERY_PER_KEY * span, loads * pair)
        done = jnp.dot(weights, value_ref[...], preferred_element_type=jnp.float32) / total
        for h in range(QUERY_PER_KEY):
            for s in range(sources):
                first = h * span + s * per_pair
                done_ref[
                    s, b * per_pair : (b + 1) * per_pair, h * HEAD_SIZE : (h + 1) * HEAD_SIZE
                ] = done[first : first + per_pair]
    out_ref[...] = done_ref[...].astype(out_ref.dtype)


def attend(starts, queries, loads, values, sources, per_pair):
    n = queries.shape[0]
    keys = len(loads) * 2 * sources * per_pair
    shape = (sources, n // sources, QUERY_WIDTH)
    return pl.pallas_call(
        functools.partial(attend_kernel, per_pair, len(loads)),
        in_specs=whole(2 + 2 * len(loads)),
        out_specs=pl.BlockSpec(memory_space=pltpu.VMEM),
        out_shape=jax.ShapeDtypeStruct(shape, queries.dtype),
        scratch_shapes=[
            pltpu.VMEM((keys, HEAD_SIZE), queries.dtype),
            pltpu.VMEM((keys, HEAD_SIZE), queries.dtype),
            pltpu.VMEM(shape, jnp.float32),
        ],
        compiler_params=params(),
        cost_estimate=cost(4 * n * keys * QUERY_WIDTH, 4 * n * QUERY_WIDTH),
        name="attend",
    )(starts, queries, *loads, *values)


def exchange(blocks, axis):
    return lax.all_to_all(blocks, axis, split_axis=0, concat_axis=0, tiled=True)


def per_device(section_token_rows, row_target, doc_lengths):
    tp_count = lax.axis_size("tp")
    slabs = lax.axis_size("zh")
    parts = lax.axis_size("x") * lax.axis_size("zl")
    local_rows = section_token_rows.shape[0]
    tok_dev = local_rows * tp_count
    per_pair = tok_dev // (parts * slabs)
    part = lax.axis_index("x") * lax.axis_size("zl") + lax.axis_index("zl")
    starts = (jnp.cumsum(doc_lengths) - doc_lengths - part * (slabs * tok_dev)).reshape(1, -1)
    starts = starts.astype(jnp.float32)

    keys = split_keys(section_token_rows, row_target, tp_count)
    keys = exchange(keys, "tp")
    keys, forward, backward = sort_rows(keys, parts, per_pair)
    load = arrange(exchange(keys, PART), per_pair)

    load, rows = lax.optimization_barrier((load, section_token_rows))
    queries = split_queries(rows, tp_count)
    queries = exchange(queries, "tp").reshape(tok_dev, QUERY_WIDTH)
    queries = permute_rows(forward, queries)
    queries = exchange(queries.reshape(parts, tok_dev // parts, QUERY_WIDTH), PART)
    queries = queries.reshape(parts, slabs, per_pair, QUERY_WIDTH).transpose(1, 0, 2, 3)
    queries = queries.reshape(tok_dev, QUERY_WIDTH)

    def passed(block, sign):
        route = []
        for at in range(slabs):
            for low in range(2):
                to = (at + sign * (1 - 2 * low)) % slabs
                route.append((at * 2 + low, to * 2 + low))
        return lax.ppermute(block, RING, route)

    loads = [load]
    load_a, load_b = load, load
    for _ in range(1, slabs // 2):
        load_a = passed(load_a, 1)
        load_b = passed(load_b, -1)
        loads += [load_a, load_b]
    last_values = passed(load_a[:, HEAD_SIZE:], 1)
    last_keys = passed(load_b[:, :HEAD_SIZE], -1)
    loads, values = loads + [last_keys], loads + [last_values]

    done = attend(starts, queries, loads, values, parts, per_pair)
    back = exchange(done, PART).reshape(tok_dev, QUERY_WIDTH)
    back = permute_rows(backward, back).reshape(tp_count, local_rows, QUERY_WIDTH)
    back = exchange(back, "tp")
    return back.transpose(1, 0, 2).reshape(local_rows, tp_count * QUERY_WIDTH)


def solution(mesh):
    shape = (4, 8, 2, mesh.shape["tp"])
    ring_mesh = Mesh(mesh.devices.reshape(shape), AXES)
    placed = (P(AXES, None), P(AXES), P())
    return jax.shard_map(
        per_device, mesh=ring_mesh, in_specs=placed, out_specs=P(AXES, None), check_vma=False
    )
```
